32 devices in a mesh: dp: 4 (over y, core), ctx: 4 (over z), tensor: 2 (over x).
Axes of the slice: x: 2, y: 2, z: 4, core: 2. Of those that a mesh axis runs over, the one named last changes fastest.
Arguments:
- layer_input: bfloat16 [4, 2048, 2304], P('dp', 'ctx'), may hold values from -6 to 6
- block_order: int32 [4, 8], P('dp'), may hold values from 0 to 7, each once within a row
- pre_attend: bfloat16 [2304], P(('dp', 'ctx')), may hold values from 0.5 to 1.5
- query_weight: bfloat16 [2304, 2048], P(('dp', 'ctx'), 'tensor'), may hold values from -0.25 to 0.25
- key_weight: bfloat16 [2304, 1024], P(('dp', 'ctx'), 'tensor'), may hold values from -0.125 to 0.125
- value_weight: bfloat16 [2304, 1024], P(('dp', 'ctx'), 'tensor'), may hold values from -0.125 to 0.125
- output_weight: bfloat16 [2048, 2304], P('tensor', ('dp', 'ctx')), may hold values from -0.125 to 0.125
- post_attend: bfloat16 [2304], P(('dp', 'ctx')), may hold values from 0.5 to 1.5
- pre_feed: bfloat16 [2304], P(('dp', 'ctx')), may hold values from 0.5 to 1.5
- gate_weight: bfloat16 [2304, 9216], P(('dp', 'ctx'), 'tensor'), may hold values from -0.125 to 0.125
- up_weight: bfloat16 [2304, 9216], P(('dp', 'ctx'), 'tensor'), may hold values from -0.125 to 0.125
- down_weight: bfloat16 [9216, 2304], P('tensor', ('dp', 'ctx')), may hold values from -0.0625 to 0.0625
- post_feed: bfloat16 [2304], P(('dp', 'ctx')), may hold values from 0.5 to 1.5
- cotangent: bfloat16 [4, 2048, 2304], P('dp', 'ctx'), may hold values from -6 to 6
Outputs:
- layer_output: bfloat16 [4, 2048, 2304], P('dp', 'ctx')
- input_grad: float32 [4, 2048, 2304], P('dp', 'ctx')
- pre_attend_grad: float32 [2304], P(('dp', 'ctx'))
- query_weight_grad: float32 [2304, 2048], P(('dp', 'ctx'), 'tensor')
- key_weight_grad: float32 [2304, 1024], P(('dp', 'ctx'), 'tensor')
- value_weight_grad: float32 [2304, 1024], P(('dp', 'ctx'), 'tensor')
- output_weight_grad: float32 [2048, 2304], P('tensor', ('dp', 'ctx'))
- post_attend_grad: float32 [2304], P(('dp', 'ctx'))
- pre_feed_grad: float32 [2304], P(('dp', 'ctx'))
- gate_weight_grad: float32 [2304, 9216], P(('dp', 'ctx'), 'tensor')
- up_weight_grad: float32 [2304, 9216], P(('dp', 'ctx'), 'tensor')
- down_weight_grad: float32 [9216, 2304], P('tensor', ('dp', 'ctx'))
- post_feed_grad: float32 [2304], P(('dp', 'ctx'))
The draws below stay inside these ranges and needn't reach their ends.
Inputs may be any that keep to these rules, and one draw needn't show every extreme that they name: Each row of block_order names every one of the 8 blocks of a sequence once.
All inputs are finite; a program needn't handle non-finite values.
Results may differ from the reference program's by a relative error of at most 0.02.
Values may be sent and summed in bfloat16 or wider, within the bound.
No kernel may reach another device: no remote copies, remote signals or barrier semaphores. Data moves between devices by JAX's collectives and lax.ppermute only.
A program may use at most 320 MiB of HBM per device.

```python
import jax
import jax.numpy as jnp
from jax import lax

D = 2304
HQ = 8
KV = 4
HD = 256
FF = 9216
LEN = 2048
SEQS = 4
BLOCKS = 8
BLOCK = 256


def block_levels(rng, shape, cuts, least, top_value):
    def one(dim, shards_of):
        steps = jax.random.uniform(jax.random.fold_in(jax.random.fold_in(rng, 6), dim), (shards_of,), jnp.float32, least / len(cuts), top_value / len(cuts))
        return jnp.repeat(jnp.exp(steps), shape[dim] // shards_of).reshape((-1,) + (1,) * (len(shape) - dim - 1))

    level = one(*cuts[0])
    for cut in cuts[1:]:
        level = level * one(*cut)
    return level


def scatter_about(key, dims, width, bound, pieces=(), held_as=jnp.bfloat16):
    factor_of = block_levels(key, dims, pieces, -0.22, 0.18) if pieces else 1.0
    values = jax.random.normal(key, dims, jnp.float32) * width * factor_of
    return jnp.minimum(jnp.maximum(values, -bound), bound).astype(held_as)


def setup_inputs(seed: int = 0) -> dict:
    streams_of = jax.random.split(jax.random.key(seed), 15)
    layer_input = scatter_about(streams_of[0], (SEQS, LEN, D), 1.0, 6.0, ((0, 4), (1, 4)))
    block_order = jax.vmap(lambda own: jax.random.permutation(own, BLOCKS))(jax.random.split(streams_of[1], SEQS)).reshape((SEQS, BLOCKS)).astype(jnp.int32)
    pre_attend = jnp.clip(1.0 + 0.1 * jax.random.normal(streams_of[2], (D,), jnp.float32), 0.5, 1.5).astype(jnp.bfloat16)
    query_weight = scatter_about(streams_of[3], (D, HQ * HD), (D // 4) ** -0.5, 0.25, ((0, 16), (1, 2)))
    key_weight = scatter_about(streams_of[4], (D, KV * HD), D ** -0.5, 0.125, ((0, 16), (1, 2)))
    value_weight = scatter_about(streams_of[5], (D, KV * HD), D ** -0.5, 0.125, ((0, 16), (1, 2)))
    output_weight = scatter_about(streams_of[6], (HQ * HD, D), (HQ * HD) ** -0.5, 0.125, ((0, 2), (1, 16)))
    post_attend = jnp.clip(1.0 + 0.1 * jax.random.normal(streams_of[7], (D,), jnp.float32), 0.5, 1.5).astype(jnp.bfloat16)
    pre_feed = jnp.clip(1.0 + 0.1 * jax.random.normal(streams_of[8], (D,), jnp.float32), 0.5, 1.5).astype(jnp.bfloat16)
    gate_weight = scatter_about(streams_of[9], (D, FF), D ** -0.5, 0.125, ((0, 16), (1, 2)))
    up_weight = scatter_about(streams_of[10], (D, FF), D ** -0.5, 0.125, ((0, 16), (1, 2)))
    down_weight = scatter_about(streams_of[11], (FF, D), FF ** -0.5, 0.0625, ((0, 2), (1, 16)))
    post_feed = jnp.clip(1.0 + 0.1 * jax.random.normal(streams_of[12], (D,), jnp.float32), 0.5, 1.5).astype(jnp.bfloat16)
    cotangent = scatter_about(streams_of[13], (SEQS, LEN, D), 1.0, 6.0, ((0, 4), (1, 4)))
    return {"layer_input": layer_input, "block_order": block_order, "pre_attend": pre_attend, "query_weight": query_weight, "key_weight": key_weight, "value_weight": value_weight, "output_weight": output_weight, "post_attend": post_attend, "pre_feed": pre_feed, "gate_weight": gate_weight, "up_weight": up_weight, "down_weight": down_weight, "post_feed": post_feed, "cotangent": cotangent}


@jax.custom_vjp
def low(v):
    return lax.optimization_barrier(v.astype(jnp.bfloat16)).astype(jnp.float32)

@jax.custom_vjp
def low_back(v):
    return v

def low_keep(v):
    return (low(v), None)

def low_pass(kept, grad):
    return (grad,)

def back_keep(v):
    return (v, None)

def back_low(kept, grad):
    return (low(grad),)
low.defvjp(low_keep, low_pass)
low_back.defvjp(back_keep, back_low)
epsilon = 1e-06
cap_value = 50.0
gelu_coef = 0.7978845608028654
masked_value = -1e+30

def rms_norm(values, gain):
    factor = lax.rsqrt(lax.optimization_barrier(jnp.mean(values * values, axis=-1, keepdims=True)) + epsilon)
    return values * factor * gain

def gelu_tanh(values):
    return 0.5 * values * (1.0 + jnp.tanh(gelu_coef * (values + 0.044715 * values * values * values)))

def gated_product(gate, upward):
    return gelu_tanh(gate) * upward

def rotary_tables(positions, head_size):
    half = head_size // 2
    freqs = 10000.0 ** (-(jnp.arange(half, dtype=jnp.float32) * 2.0) / head_size)
    angle = positions.astype(jnp.float32)[:, None] * freqs[None, :]
    return (jnp.cos(angle), jnp.sin(angle))

def rotate(values, cosine, sine):
    half = values.shape[-1] // 2
    first = values[..., :half]
    second = values[..., half:]
    cosine = cosine[:, None, :]
    sine = sine[:, None, :]
    return jnp.concatenate([first * cosine - second * sine, second * cosine + first * sine], axis=-1)

def attend_probs(raw, visible):
    capped = cap_value * jnp.tanh(raw / cap_value)
    capped = jnp.where(visible, capped, masked_value)
    return jax.nn.softmax(capped, axis=-1)

def matmul(left, right):
    return jnp.dot(left, right, precision=lax.Precision.HIGHEST)

def layer_sequence(seq_input, order_row, pre_attend, query_weight, key_weight, value_weight, output_weight, post_attend, pre_feed, gate_weight, up_weight, down_weight, post_feed):
    positions = (order_row[:, None] * BLOCK + jnp.arange(BLOCK, dtype=jnp.int32)[None, :]).reshape(LEN)
    cosine, sine = rotary_tables(positions, HD)
    visible = positions[:, None] >= positions[None, :]
    attend_in = low(rms_norm(seq_input, pre_attend))
    query_pre = low_back(matmul(attend_in, query_weight)).reshape(LEN, HQ, HD)
    key_pre = low_back(matmul(attend_in, key_weight)).reshape(LEN, KV, HD)
    values = low(low_back(matmul(attend_in, value_weight))).reshape(LEN, KV, HD)
    queries = low(rotate(query_pre, cosine, sine)).reshape(LEN, KV, HQ // KV, HD)
    keys = low(rotate(key_pre, cosine, sine))
    raw = low_back(jnp.einsum('qgrd,kgd->grqk', queries, keys, precision=lax.Precision.HIGHEST) * HD ** (-0.5))
    probs = low(attend_probs(raw, visible))
    attended = jnp.einsum('grqk,kgd->qgrd', probs, values, precision=lax.Precision.HIGHEST).reshape(LEN, HQ * HD)
    attended = low(low_back(attended))
    attend_out = low_back(matmul(attended, output_weight))
    hidden_mid = seq_input + rms_norm(attend_out, post_attend)
    feed_in = low(rms_norm(hidden_mid, pre_feed))
    gate = low_back(matmul(feed_in, gate_weight))
    upward = low_back(matmul(feed_in, up_weight))
    mixed = low(gated_product(gate, upward))
    feed_out = low_back(matmul(mixed, down_weight))
    return hidden_mid + rms_norm(feed_out, post_feed)

def reference(layer_input, block_order, pre_attend, query_weight, key_weight, value_weight, output_weight, post_attend, pre_feed, gate_weight, up_weight, down_weight, post_feed, cotangent):
    primals = tuple((item.astype(jnp.float32) for item in (layer_input, pre_attend, query_weight, key_weight, value_weight, output_weight, post_attend, pre_feed, gate_weight, up_weight, down_weight, post_feed)))

    def forward(inputs, *weights):

        def one_sequence(carry, item):
            seq_input, order_row = item
            return (carry, jax.checkpoint(layer_sequence)(seq_input, order_row, *weights))
        _, result = lax.scan(one_sequence, jnp.zeros((), jnp.float32), (inputs, block_order))
        return result
    result, backward = jax.vjp(forward, *primals)
    grads = backward(cotangent.astype(jnp.float32))
    return (result.astype(jnp.bfloat16), grads[0], grads[1], grads[2], grads[3], grads[4], grads[5], grads[6], grads[7], grads[8], grads[9], grads[10], grads[11])
```

```python
import jax
import jax.numpy as jnp
from jax import lax
from jax.sharding import PartitionSpec as P

HQ = 8
KV = 4
HD = 256
LEN = 2048

epsilon = 1e-06
cap_value = 50.0
gelu_coef = 0.7978845608028654
masked_value = -1e30
cores = 2
pad_lanes = 128

f32 = jnp.float32
bf16 = jnp.bfloat16


def rms_norm(values, gain):
    factor = lax.rsqrt(jnp.mean(values * values, axis=-1, keepdims=True) + epsilon)
    return values * factor * gain


def gelu_tanh(values):
    return (
        0.5 * values * (1.0 + jnp.tanh(gelu_coef * (values + 0.044715 * values * values * values)))
    )


def gated_product(gate, upward):
    return gelu_tanh(gate) * upward


def rotary_tables(positions, head_size):
    half = head_size // 2
    freqs = 10000.0 ** (-(jnp.arange(half, dtype=f32) * 2.0) / head_size)
    angle = positions.astype(f32)[:, None] * freqs[None, :]
    return (jnp.cos(angle), jnp.sin(angle))


def rotate(values, cosine, sine):
    half = values.shape[-1] // 2
    first = values[..., :half]
    second = values[..., half:]
    cosine = cosine[:, None, :]
    sine = sine[:, None, :]
    return jnp.concatenate(
        [first * cosine - second * sine, second * cosine + first * sine], axis=-1
    )


def unrotate(grads, cosine, sine):
    half = grads.shape[-1] // 2
    first = grads[..., :half]
    second = grads[..., half:]
    cosine = cosine[:, None, :]
    sine = sine[:, None, :]
    return jnp.concatenate(
        [first * cosine + second * sine, second * cosine - first * sine], axis=-1
    )


def attend_probs(raw, visible):
    capped = cap_value * jnp.tanh(raw / cap_value)
    capped = jnp.where(visible, capped, masked_value)
    return jax.nn.softmax(capped, axis=-1)


def contract(left, right, left_dim, right_dim):
    return lax.dot_general(
        left, right, (((left_dim,), (right_dim,)), ((), ())), preferred_element_type=f32
    )


def body(
    layer_input,
    block_order,
    pre_attend,
    query_weight,
    key_weight,
    value_weight,
    output_weight,
    post_attend,
    pre_feed,
    gate_weight,
    up_weight,
    down_weight,
    post_feed,
    cotangent,
):
    _, rows, width = layer_input.shape
    block_len = LEN // block_order.shape[1]
    per_group = HQ // KV
    tensor_count = lax.axis_size("tensor")
    groups = KV // tensor_count
    factor = HD ** (-0.5)
    dp_count = lax.axis_size("dp")
    ctx_count = lax.axis_size("ctx")
    tensor_index = lax.axis_index("tensor")
    ctx_index = lax.axis_index("ctx")
    dp_index = lax.axis_index("dp")
    y_count = dp_count // cores
    y_index = dp_index // cores
    core_index = dp_index % cores
    share = width // (dp_count * ctx_count)
    quarter = share * ctx_count
    half = rows // tensor_count
    x_swap = [(0, 1), (1, 0)]

    def relative(values):
        first, second = values[:half], values[half:]
        flip = tensor_index == 1
        return jnp.concatenate(
            [jnp.where(flip, second, first), jnp.where(flip, first, second)], axis=0
        )

    def join(own):
        return jnp.concatenate([own, lax.ppermute(own, "tensor", x_swap)], axis=0)

    def join_absolute(own):
        return relative(join(own))

    def sum_half(left, right, left_dim, right_dim):
        other = contract(left[half:], right, left_dim, right_dim).astype(bf16)
        got = lax.ppermute(other, "tensor", x_swap)
        return contract(left[:half], right, left_dim, right_dim) + got.astype(f32)

    all_pos = (
        block_order[0][:, None] * block_len + jnp.arange(block_len, dtype=jnp.int32)[None, :]
    ).reshape(ctx_count, tensor_count, half)
    all_pos = jnp.where(tensor_index == 1, all_pos[:, ::-1], all_pos).reshape(ctx_count, rows)
    source = (ctx_index - jnp.arange(ctx_count, dtype=jnp.int32)) % ctx_count
    key_pos = jnp.take(all_pos, source, axis=0)
    local_pos = key_pos[0]
    key_pos = key_pos.reshape(LEN)
    cosine, sine = rotary_tables(local_pos, HD)
    visible = local_pos[:, None] >= key_pos[None, :]

    gain_pack = jnp.stack([pre_attend, post_attend, pre_feed, post_feed], axis=1)
    gain_pack = jnp.pad(gain_pack, ((0, 0), (0, pad_lanes - 4)))
    first_pack = jnp.concatenate([query_weight, key_weight, value_weight, gain_pack], axis=1)
    both = ("dp", "ctx")
    first_all = lax.all_gather(first_pack, both, axis=0, tiled=True)
    out_mat = lax.all_gather(output_weight.T, both, axis=0, tiled=True)
    gate_mat = lax.all_gather(gate_weight, both, axis=0, tiled=True)
    up_mat = lax.all_gather(up_weight, both, axis=0, tiled=True)
    down_mat = lax.all_gather(down_weight.T, both, axis=0, tiled=True)

    query_width = query_weight.shape[1]
    key_width = key_weight.shape[1]
    attend_width = query_width + 2 * key_width
    attend_mat = first_all[:, :attend_width]
    gains = first_all[:, attend_width : attend_width + 8].T.astype(f32)
    gain_in, gain_out, feed_gain, feed_post = gains[0], gains[1], gains[2], gains[3]

    inputs = relative(layer_input[0].astype(f32))
    own_inputs = inputs[:half]
    cot = lax.dynamic_slice_in_dim(cotangent[0], tensor_index * half, half, 0).astype(f32)

    attend_in = rms_norm(inputs, gain_in).astype(bf16)
    projected = jnp.dot(attend_in, attend_mat, preferred_element_type=f32)
    query_pre = projected[:, :query_width]
    key_pre = projected[:, query_width : query_width + key_width]
    value_pre = projected[:, query_width + key_width :]
    keys_local = (
        rotate(key_pre.reshape(rows, groups, HD), cosine, sine).astype(bf16).reshape(rows, -1)
    )
    values_local = value_pre.astype(bf16)
    kv_local = jnp.concatenate([keys_local, values_local], axis=1)
    kv_parts = [kv_local]
    for step in range(1, ctx_count):
        pairs = [(i, (i + step) % ctx_count) for i in range(ctx_count)]
        kv_parts.append(lax.ppermute(kv_local, "ctx", pairs))
    kv_all = jnp.concatenate(kv_parts, axis=0)
    key_heads = kv_all[:, :key_width].reshape(LEN, groups, HD)
    value_heads = kv_all[:, key_width:].reshape(LEN, groups, HD)
    queries = (
        rotate(query_pre.reshape(rows, -1, HD), cosine, sine)
        .astype(bf16)
        .reshape(rows, groups, per_group, HD)
    )

    raw = (
        jnp.einsum("qgrd,kgd->grqk", queries, key_heads, preferred_element_type=f32) * factor
    )
    probs, prob_back = jax.vjp(lambda inner: attend_probs(inner, visible), raw)
    probs_low = probs.astype(bf16)
    attended = (
        jnp.einsum("grqk,kgd->qgrd", probs_low, value_heads, preferred_element_type=f32)
        .astype(bf16)
        .reshape(rows, -1)
    )
    attend_out = sum_half(attended, out_mat, 1, 1)
    hidden_mid = own_inputs + rms_norm(attend_out, gain_out)
    feed_in = join(rms_norm(hidden_mid, feed_gain).astype(bf16))
    gate = jnp.dot(feed_in, gate_mat, preferred_element_type=f32)
    upward = jnp.dot(feed_in, up_mat, preferred_element_type=f32)
    mixed = gated_product(gate, upward).astype(bf16)
    feed_out = sum_half(mixed, down_mat, 1, 1)
    layer_output = join_absolute(
        (hidden_mid + rms_norm(feed_out, feed_post)).astype(bf16)
    )[None]

    def pick(matrix, dy, dc):
        index = ((y_index + dy) % y_count) * cores + (core_index + dc) % cores
        return lax.dynamic_slice_in_dim(matrix, index * quarter, quarter, 1)

    def along(dy, dc):
        pairs = []
        for y in range(y_count):
            for core in range(cores):
                target = ((y + dy) % y_count) * cores + (core + dc) % cores
                pairs.append((y * cores + core, target))
        return pairs

    def reduce_rows(left, right, extra=None):
        def piece(dy, dc):
            result = contract(pick(left, dy, dc), right, 0, 0)
            if extra is not None:
                result = jnp.concatenate([result, pick(extra, dy, dc).T], axis=1)
            return result

        swapped = [
            lax.ppermute(piece(dy, 1).astype(bf16), "dp", along(0, 1)) for dy in range(y_count)
        ]
        total = piece(0, 0) + swapped[0].astype(f32)
        arrived = []
        for dy in range(1, y_count):
            partial = (piece(dy, 0) + swapped[dy].astype(f32)).astype(bf16)
            arrived.append(lax.ppermute(partial, "dp", along(dy, 0)))
        for item in arrived:
            total = total + item.astype(f32)
        return lax.psum_scatter(
            total.astype(bf16), "ctx", scatter_dimension=0, tiled=True
        ).astype(f32)

    def norm_back(values, gain, incoming):
        _, back = jax.vjp(rms_norm, values, gain)
        return back(incoming)

    d_feed_out, post_feed_part = norm_back(feed_out, feed_post, cot)
    d_feed_low = join(d_feed_out.astype(bf16))
    down_grad = reduce_rows(d_feed_low, mixed).T
    d_mixed = jnp.dot(d_feed_low, down_mat, preferred_element_type=f32)
    _, gate_back = jax.vjp(gated_product, gate, upward)
    d_gate, d_upward = gate_back(d_mixed)
    d_gate = d_gate.astype(bf16)
    d_upward = d_upward.astype(bf16)

    other = (
        contract(d_gate[half:], gate_mat, 1, 1) + contract(d_upward[half:], up_mat, 1, 1)
    ).astype(bf16)
    got = lax.ppermute(other, "tensor", x_swap)
    d_feed_in = (
        contract(d_gate[:half], gate_mat, 1, 1)
        + contract(d_upward[:half], up_mat, 1, 1)
        + got.astype(f32)
    )
    gate_grad = reduce_rows(feed_in, d_gate)
    up_grad = reduce_rows(feed_in, d_upward)

    d_from_feed, pre_feed_part = norm_back(hidden_mid, feed_gain, d_feed_in)
    d_mid = cot + d_from_feed
    d_attend_out, post_attend_part = norm_back(attend_out, gain_out, d_mid)
    d_attend_low = join(d_attend_out.astype(bf16))
    d_attended = (
        jnp.dot(d_attend_low, out_mat, preferred_element_type=f32)
        .astype(bf16)
        .reshape(rows, groups, per_group, HD)
    )
    d_probs = jnp.einsum("qgrd,kgd->grqk", d_attended, value_heads, preferred_element_type=f32)
    d_raw = prob_back(d_probs)[0].astype(bf16)
    d_query = jnp.einsum("grqk,kgd->qgrd", d_raw, key_heads, preferred_element_type=f32) * factor
    d_key = jnp.einsum("grqk,qgrd->kgd", d_raw, queries, preferred_element_type=f32) * factor
    d_value = jnp.einsum("grqk,qgrd->kgd", probs_low, d_attended, preferred_element_type=f32)
    d_kv = jnp.concatenate([d_key.reshape(LEN, -1), d_value.reshape(LEN, -1)], axis=1)
    d_kv_local = d_kv[:rows]
    for step in range(1, ctx_count):
        pairs = [(i, (i - step) % ctx_count) for i in range(ctx_count)]
        sent = d_kv[step * rows : (step + 1) * rows].astype(bf16)
        d_kv_local = d_kv_local + lax.ppermute(sent, "ctx", pairs).astype(f32)
    d_query_pre = (
        unrotate(d_query.reshape(rows, -1, HD), cosine, sine).reshape(rows, -1).astype(bf16)
    )
    d_key_pre = (
        unrotate(d_kv_local[:, :key_width].reshape(rows, groups, HD), cosine, sine)
        .reshape(rows, -1)
        .astype(bf16)
    )
    d_value_pre = d_kv_local[:, key_width:].astype(bf16)
    d_projected = jnp.concatenate([d_query_pre, d_key_pre, d_value_pre], axis=1)
    d_attend_part = contract(d_projected, attend_mat, 1, 1)

    in_factor = lax.rsqrt(jnp.mean(inputs * inputs, axis=-1, keepdims=True) + epsilon)
    pre_attend_part = jnp.sum(d_attend_part * inputs * in_factor, axis=0)
    gain_parts = jnp.stack([pre_attend_part, post_attend_part, pre_feed_part, post_feed_part])
    gain_parts = jnp.pad(gain_parts, ((0, pad_lanes - 4), (0, 0)))

    out_grad = reduce_rows(d_attend_low, attended).T
    attend_grad = reduce_rows(attend_in, d_projected, gain_parts)
    query_grad = attend_grad[:, :query_width]
    key_grad = attend_grad[:, query_width : query_width + key_width]
    value_grad = attend_grad[:, query_width + key_width : attend_width]
    gain_grads = attend_grad[:, attend_width:]
    gain_grads = (gain_grads + lax.ppermute(gain_grads, "tensor", x_swap)).T

    got = lax.ppermute(d_attend_part[half:].astype(bf16), "tensor", x_swap)
    d_attend_in = d_attend_part[:half] + got.astype(f32)
    d_from_attend, _ = norm_back(own_inputs, gain_in, d_attend_in)
    input_grad = join_absolute((d_mid + d_from_attend).astype(bf16)).astype(f32)[None]

    return (
        layer_output,
        input_grad,
        gain_grads[0],
        query_grad,
        key_grad,
        value_grad,
        out_grad,
        gain_grads[1],
        gain_grads[2],
        gate_grad,
        up_grad,
        down_grad,
        gain_grads[3],
    )


def solution(mesh):
    both = ("dp", "ctx")
    return jax.shard_map(
        body,
        mesh=mesh,
        in_specs=(
            P("dp", "ctx", None),
            P("dp", None),
            P(both),
            P(both, "tensor"),
            P(both, "tensor"),
            P(both, "tensor"),
            P("tensor", both),
            P(both),
            P(both),
            P(both, "tensor"),
            P(both, "tensor"),
            P("tensor", both),
            P(both),
            P("dp", "ctx", None),
        ),
        out_specs=(
            P("dp", "ctx", None),
            P("dp", "ctx", None),
            P(both),
            P(both, "tensor"),
            P(both, "tensor"),
            P(both, "tensor"),
            P("tensor", both),
            P(both),
            P(both),
            P(both, "tensor"),
            P(both, "tensor"),
            P("tensor", both),
            P(both),
        ),
        check_vma=False,
    )
```

```python
import functools

import jax
import jax.numpy as jnp
from jax import lax
from jax.experimental import pallas as pl
from jax.experimental.pallas import tpu as pltpu
from jax.sharding import PartitionSpec as P

HQ = 8
KV = 4
HD = 256
LEN = 2048

epsilon = 1e-06
cap_value = 50.0
gelu_coef = 0.7978845608028654
cores = 2
pad_lanes = 128

f32 = jnp.float32
bf16 = jnp.bfloat16


def rms_norm(values, gain):
    factor = lax.rsqrt(jnp.mean(values * values, axis=-1, keepdims=True) + epsilon)
    return values * factor * gain


def gelu_tanh(values):
    return (
        0.5 * values * (1.0 + jnp.tanh(gelu_coef * (values + 0.044715 * values * values * values)))
    )


def gated_product(gate, upward):
    return gelu_tanh(gate) * upward


def rotary_tables(positions, head_size):
    half = head_size // 2
    freqs = 10000.0 ** (-(jnp.arange(half, dtype=f32) * 2.0) / head_size)
    angle = positions.astype(f32)[:, None] * freqs[None, :]
    return (jnp.cos(angle), jnp.sin(angle))


attend_limit = 48 * 1024 * 1024


def dotted(left, right, left_dim, right_dim, precision=None):
    return lax.dot_general(
        left,
        right,
        (((left_dim,), (right_dim,)), ((), ())),
        precision=precision,
        preferred_element_type=f32,
    )


def turn(values, cosine, sine):
    half = HD // 2
    first, second = values[:, :half], values[:, half:]
    return jnp.concatenate(
        [first * cosine - second * sine, second * cosine + first * sine], axis=1
    )


def forward_kernel(chunks, pre_ref, kv_ref, cos_ref, sin_ref, qpos_ref, kpos_ref, q_ref, out_ref, low_ref, inv_ref):
    rows = pre_ref.shape[0]
    size = kv_ref.shape[0] // chunks
    q = turn(pre_ref[...], cos_ref[...], sin_ref[...]).astype(bf16)
    q_ref[...] = q
    qpos = qpos_ref[...]
    total = jnp.zeros((1, rows), f32)
    acc = jnp.zeros((HD, rows), f32)
    for c in range(chunks):
        part = pl.ds(c * size, size)
        raw = dotted(kv_ref[part, :HD], q, 1, 1)
        level = jnp.tanh(raw * (HD ** (-0.5) / cap_value))
        weight = jnp.where(qpos >= kpos_ref[part, :], jnp.exp(cap_value * level), 0.0)
        total = total + jnp.sum(weight, axis=0, keepdims=True)
        acc = acc + dotted(kv_ref[part, HD:], weight.astype(bf16), 0, 0)
    inverse = 1.0 / total
    inv_ref[0] = inverse
    out = (acc * inverse).T
    out_ref[...] = out
    low_ref[...] = out.astype(bf16)


def attend_forward(query_pre, kv_all, cosine, sine, qpos, kpos, groups, per_group, chunks):
    rows, width = query_pre.shape
    length = kv_all.shape[0]
    heads = groups * per_group
    by_head = pl.BlockSpec((rows, HD), lambda g, r: (0, g * per_group + r))
    fixed = lambda shape: pl.BlockSpec(shape, lambda g, r: (0, 0))
    return pl.pallas_call(
        functools.partial(forward_kernel, chunks),
        grid=(groups, per_group),
        in_specs=[
            by_head,
            pl.BlockSpec((length, 2 * HD), lambda g, r: (0, g)),
            fixed((rows, HD // 2)),
            fixed((rows, HD // 2)),
            fixed((1, rows)),
            fixed((length, 1)),
        ],
        out_specs=[
            by_head,
            by_head,
            by_head,
            pl.BlockSpec((1, 1, rows), lambda g, r: (g * per_group + r, 0, 0)),
        ],
        out_shape=[
            jax.ShapeDtypeStruct((rows, width), bf16),
            jax.ShapeDtypeStruct((rows, width), f32),
            jax.ShapeDtypeStruct((rows, width), bf16),
            jax.ShapeDtypeStruct((heads, 1, rows), f32),
        ],
        compiler_params=pltpu.CompilerParams(vmem_limit_bytes=attend_limit),
        cost_estimate=pl.CostEstimate(
            flops=4 * rows * length * width,
            bytes_accessed=14 * rows * width + 4 * length * groups * HD,
            transcendentals=2 * rows * length * heads,
        ),
        name="attend_forward",
    )(query_pre, kv_all, cosine, sine, qpos, kpos)


def backward_kernel(per_group, q_ref, kv_ref, da_ref, out_ref, inv_ref, cos_ref, sin_ref, qpos_ref, kpos_ref, dq_ref, dkv_ref, delta_ref, sum_ref):
    c, r = pl.program_id(1), pl.program_id(2)
    q, da = q_ref[...], da_ref[...]
    k, v = kv_ref[:, :HD], kv_ref[:, HD:]

    @pl.when(c == 0)
    def _():
        delta_ref[r] = dotted(
            jnp.ones((8, HD), f32), da.astype(f32) * out_ref[...], 1, 1, lax.Precision.HIGHEST
        )

    delta = delta_ref[r][0:1]
    level = jnp.tanh(dotted(k, q, 1, 1) * (HD ** (-0.5) / cap_value))
    seen = qpos_ref[...] >= kpos_ref[...]
    prob = jnp.where(seen, jnp.exp(cap_value * level), 0.0) * inv_ref[0]
    d_prob = dotted(v, da, 1, 1)
    d_raw = (prob * (d_prob - delta) * (1.0 - level * level)).astype(bf16)
    d_key = dotted(d_raw, q, 1, 0) * HD ** (-0.5)
    d_value = dotted(prob.astype(bf16), da, 1, 0)
    d_query = dotted(d_raw, k, 0, 0)

    @pl.when(r == 0)
    def _():
        dkv_ref[:, :HD] = d_key
        dkv_ref[:, HD:] = d_value

    @pl.when(r > 0)
    def _():
        dkv_ref[:, :HD] += d_key
        dkv_ref[:, HD:] += d_value

    @pl.when(c == 0)
    def _():
        sum_ref[r] = d_query

    @pl.when(c > 0)
    def _():
        sum_ref[r] += d_query

    for head in range(per_group):

        @pl.when((c == pl.num_programs(1) - 1) & (r == head))
        def _():
            whole = sum_ref[head] * HD ** (-0.5)
            dq_ref[:, head * HD : (head + 1) * HD] = turn(
                whole, cos_ref[...], -sin_ref[...]
            ).astype(bf16)


def attend_backward(queries, kv_all, d_attended, out, inverse, cosine, sine, qpos, kpos, groups, per_group, chunks):
    rows, width = queries.shape
    length = kv_all.shape[0]
    size = length // chunks
    heads = groups * per_group
    by_head = pl.BlockSpec((rows, HD), lambda g, c, r: (0, g * per_group + r))
    fixed = lambda shape: pl.BlockSpec(shape, lambda g, c, r: (0, 0))
    by_chunk = pl.BlockSpec((size, 2 * HD), lambda g, c, r: (c, g))
    return pl.pallas_call(
        functools.partial(backward_kernel, per_group),
        grid=(groups, chunks, per_group),
        in_specs=[
            by_head,
            by_chunk,
            by_head,
            by_head,
            pl.BlockSpec((1, 1, rows), lambda g, c, r: (g * per_group + r, 0, 0)),
            fixed((rows, HD // 2)),
            fixed((rows, HD // 2)),
            fixed((1, rows)),
            pl.BlockSpec((size, 1), lambda g, c, r: (c, 0)),
        ],
        out_specs=[
            pl.BlockSpec((rows, per_group * HD), lambda g, c, r: (0, g)),
            by_chunk,
        ],
        out_shape=[
            jax.ShapeDtypeStruct((rows, width), bf16),
            jax.ShapeDtypeStruct((length, groups * 2 * HD), f32),
        ],
        scratch_shapes=[
            pltpu.VMEM((per_group, 8, rows), f32),
            pltpu.VMEM((per_group, rows, HD), f32),
        ],
        compiler_params=pltpu.CompilerParams(vmem_limit_bytes=attend_limit),
        cost_estimate=pl.CostEstimate(
            flops=10 * rows * length * width,
            bytes_accessed=10 * rows * width + 12 * length * groups * HD,
            transcendentals=2 * rows * length * heads,
        ),
        name="attend_backward",
    )(queries, kv_all, d_attended, out, inverse, cosine, sine, qpos, kpos)


def contract(left, right, left_dim, right_dim):
    return lax.dot_general(
        left, right, (((left_dim,), (right_dim,)), ((), ())), preferred_element_type=f32
    )


def body(
    layer_input,
    block_order,
    pre_attend,
    query_weight,
    key_weight,
    value_weight,
    output_weight,
    post_attend,
    pre_feed,
    gate_weight,
    up_weight,
    down_weight,
    post_feed,
    cotangent,
):
    _, rows, width = layer_input.shape
    block_len = LEN // block_order.shape[1]
    per_group = HQ // KV
    tensor_count = lax.axis_size("tensor")
    groups = KV // tensor_count
    factor = HD ** (-0.5)
    dp_count = lax.axis_size("dp")
    ctx_count = lax.axis_size("ctx")
    tensor_index = lax.axis_index("tensor")
    ctx_index = lax.axis_index("ctx")
    dp_index = lax.axis_index("dp")
    y_count = dp_count // cores
    y_index = dp_index // cores
    core_index = dp_index % cores
    share = width // (dp_count * ctx_count)
    quarter = share * ctx_count
    half = rows // tensor_count
    pair = 2
    far_count = ctx_count // pair
    far_index = ctx_index // pair
    near_index = ctx_index % pair
    x_swap = [(0, 1), (1, 0)]
    all_swaps = {}
    for bz, bx in ((0, 1), (1, 0), (1, 1)):
        all_swaps[bz, bx] = [
            (c * 2 + t, (c ^ bz) * 2 + (t ^ bx)) for c in range(ctx_count) for t in range(2)
        ]
    near_swap = [(c, c ^ 1) for c in range(ctx_count)]

    def far_shift(step):
        return [
            (c, ((c // pair + step) % far_count) * pair + c % pair) for c in range(ctx_count)
        ]

    def along(dy, dc):
        pairs = []
        for y in range(y_count):
            for core in range(cores):
                target = ((y + dy) % y_count) * cores + (core + dc) % cores
                pairs.append((y * cores + core, target))
        return pairs

    def after(value, *others):
        return lax.optimization_barrier((value, *others))[0]

    def chosen(parts, index, place):
        count = len(parts)
        result = parts[0]
        for step in range(1, count):
            result = jnp.where((index - place) % count == step, parts[step], result)
        return result

    def in_order(parts, index):
        return jnp.concatenate([chosen(parts, index, k) for k in range(len(parts))], axis=0)

    def relative(values):
        first, second = values[:half], values[half:]
        flip = tensor_index == 1
        return jnp.concatenate(
            [jnp.where(flip, second, first), jnp.where(flip, first, second)], axis=0
        )

    def join(own):
        return jnp.concatenate([own, lax.ppermute(own, "tensor", x_swap)], axis=0)

    def join_absolute(own):
        return relative(join(own))

    def join_all(own):
        parts = [own]
        for pairs in all_swaps.values():
            parts.append(lax.ppermute(own, ("ctx", "tensor"), pairs))
        return jnp.concatenate(parts, axis=0)

    def pack_all(product):
        return [product[(k + 1) * half : (k + 2) * half].astype(bf16) for k in range(3)]

    def send_all(parts):
        return [
            lax.ppermute(part, ("ctx", "tensor"), pairs)
            for part, pairs in zip(parts, all_swaps.values())
        ]

    def sum_of(own, parts):
        for item in parts:
            own = own + item.astype(f32)
        return own

    all_pos = (
        block_order[0][:, None] * block_len + jnp.arange(block_len, dtype=jnp.int32)[None, :]
    ).reshape(ctx_count, tensor_count, half)
    all_pos = jnp.where(tensor_index == 1, all_pos[:, ::-1], all_pos).reshape(ctx_count, rows)
    source = (ctx_index - jnp.arange(ctx_count, dtype=jnp.int32)) % ctx_count
    key_pos = jnp.take(all_pos, source, axis=0)
    local_pos = key_pos[0]
    cosine, sine = rotary_tables(local_pos, HD)
    query_places = local_pos[None, :]
    key_places = key_pos.reshape(LEN, 1)

    both = ("dp", "ctx")
    gain_pack = jnp.stack([pre_attend, post_attend, pre_feed, post_feed], axis=1)
    gain_pack = jnp.pad(gain_pack, ((0, 0), (0, pad_lanes - 4)))
    heads_in_turn = []
    for g in range(groups):
        heads_in_turn += [
            key_weight[:, g * HD : (g + 1) * HD],
            value_weight[:, g * HD : (g + 1) * HD],
        ]
    keyvalue_pack = jnp.concatenate([*heads_in_turn, gain_pack], axis=1)
    keyvalue_all = lax.all_gather(keyvalue_pack, both, axis=0, tiled=True)
    query_mat = lax.all_gather(query_weight, both, axis=0, tiled=True)
    out_mat = lax.all_gather(output_weight.T, both, axis=0, tiled=True)

    hidden = gate_weight.shape[1] // pair
    is_high = near_index == 1

    def split(weight):
        low, high = weight[:, :hidden], weight[:, hidden:]
        return jnp.where(is_high, high, low), jnp.where(is_high, low, high)

    def far_pack(mine, got):
        return jnp.concatenate(
            [jnp.where(is_high, got, mine), jnp.where(is_high, mine, got)], axis=0
        )

    def far_start(block):
        return [lax.ppermute(block, "ctx", far_shift(s)) for s in range(1, far_count)]

    gate_mine, gate_other = split(gate_weight)
    up_mine, up_other = split(up_weight)
    down_mine, down_other = split(down_weight.T)
    gate_got = lax.ppermute(gate_other, "ctx", near_swap)
    rest_got = lax.ppermute(jnp.concatenate([up_other, down_other], axis=0), "ctx", near_swap)
    gate_block = far_pack(gate_mine, gate_got)
    gate_far = far_start(gate_block)
    up_block = far_pack(up_mine, rest_got[: rest_got.shape[0] // 2])
    down_block = far_pack(down_mine, rest_got[rest_got.shape[0] // 2 :])

    keyvalue_width = 2 * key_weight.shape[1]
    keyvalue_all = after(keyvalue_all, up_block, down_block)
    keyvalue_mat = keyvalue_all[:, :keyvalue_width]
    gains = keyvalue_all[:, keyvalue_width : keyvalue_width + 8].T.astype(f32)
    gain_in, gain_out, feed_gain, feed_post = gains[0], gains[1], gains[2], gains[3]

    inputs = relative(layer_input[0].astype(f32))
    own_inputs = inputs[:half]
    cot = lax.dynamic_slice_in_dim(cotangent[0], tensor_index * half, half, 0).astype(f32)

    attend_in = rms_norm(inputs, gain_in).astype(bf16)
    keyvalue_pre = jnp.dot(attend_in, keyvalue_mat, preferred_element_type=f32)
    turned = []
    for g in range(groups):
        middle = (2 * g + 1) * HD
        turned += [
            turn(keyvalue_pre[:, middle - HD : middle], cosine, sine),
            keyvalue_pre[:, middle : middle + HD],
        ]
    kv_local = jnp.concatenate(turned, axis=1).astype(bf16)

    from_left, from_right = [kv_local], [kv_local]

    def line_step(step, left_block, right_block):
        right_pairs = [(i, i + 1) for i in range(step - 1, ctx_count - 1)]
        left_pairs = [(i, i - 1) for i in range(1, ctx_count - step + 1)]
        from_left.append(lax.ppermute(left_block, "ctx", right_pairs))
        from_right.append(lax.ppermute(right_block, "ctx", left_pairs))

    line_step(1, kv_local, kv_local)
    gate_far = [after(part, kv_local) for part in gate_far]
    gate_rows = in_order([gate_block] + gate_far, far_index)
    gate_mat = lax.all_gather(gate_rows, "dp", axis=0, tiled=True)
    up_far = far_start(after(up_block, gate_rows))
    for step in range(2, ctx_count):
        left_block, right_block = from_left[-1], from_right[-1]
        if step == 2:
            left_block, right_block = after(left_block, gate_rows), after(right_block, gate_rows)
        line_step(step, left_block, right_block)
    last_blocks = (from_left[-2], from_right[-2])
    query_pre = jnp.dot(
        after(attend_in, *last_blocks), query_mat, preferred_element_type=f32
    )
    kv_parts = [kv_local]
    for step in range(1, ctx_count):
        kv_parts.append(
            jnp.where(ctx_index >= step, from_left[step], from_right[ctx_count - step])
        )
    kv_all = jnp.concatenate(kv_parts, axis=0)
    up_far = [after(part, *last_blocks) for part in up_far]
    up_rows = in_order([up_block] + up_far, far_index)
    up_mat = lax.all_gather(up_rows, "dp", axis=0, tiled=True)
    down_far = far_start(after(down_block, up_rows))
    kv_all = after(kv_all, up_rows)
    queries, attended_wide, attended, inverse_sums = attend_forward(
        query_pre, kv_all, cosine, sine, query_places, key_places, groups, per_group, ctx_count
    )
    down_far = [after(part, attended) for part in down_far]
    down_rows = in_order([down_block] + down_far, far_index)
    down_mat = lax.all_gather(down_rows, "dp", axis=0, tiled=True)
    other = contract(attended[half:], out_mat, 1, 1).astype(bf16)
    got = after(lax.ppermute(other, "tensor", x_swap), down_rows)
    attend_out = contract(attended[:half], out_mat, 1, 1) + got.astype(f32)
    hidden_mid = own_inputs + rms_norm(attend_out, gain_out)
    feed_own = rms_norm(hidden_mid, feed_gain).astype(bf16)
    feed_in = join_all(feed_own)
    gate = jnp.dot(feed_in, gate_mat, preferred_element_type=f32)
    upward = jnp.dot(feed_in, up_mat, preferred_element_type=f32)
    mixed = gated_product(gate, upward).astype(bf16)
    feed_part = contract(mixed, down_mat, 1, 1)
    sent = send_all(pack_all(feed_part))
    feed_out = sum_of(feed_part[:half], sent)
    layer_output = join_absolute(
        (hidden_mid + rms_norm(feed_out, feed_post)).astype(bf16)
    )[None]

    class Reduction:
        def __init__(self, left, right, extra=None):
            result = contract(left, right, 0, 0).astype(bf16)
            if extra is not None:
                result = jnp.concatenate([result, extra.T.astype(bf16)], axis=1)
            self.whole = result

        def piece(self, dy, dc):
            index = ((y_index + dy) % y_count) * cores + (core_index + dc) % cores
            return lax.dynamic_slice_in_dim(self.whole, index * quarter, quarter, 0)

        def core_pack(self):
            self.packed = [self.piece(dy, 1) for dy in range(y_count)]
            return self.packed

        def core_send(self):
            self.swapped = [lax.ppermute(p, "dp", along(0, 1)) for p in self.packed]

        def y_pack(self, *before):
            swapped = self.swapped
            if before:
                swapped = [after(item, *before) for item in swapped]
            self.packed = [
                (self.piece(dy, 0).astype(f32) + swapped[dy].astype(f32)).astype(bf16)
                for dy in range(1, y_count)
            ]
            return self.packed

        def y_send(self):
            self.arrived = [
                lax.ppermute(p, "dp", along(dy + 1, 0)) for dy, p in enumerate(self.packed)
            ]

        def column(self):
            total = self.piece(0, 0).astype(f32) + self.swapped[0].astype(f32)
            return sum_of(total, self.arrived)

        def finish_ctx(self):
            return lax.psum_scatter(
                self.column().astype(bf16), "ctx", scatter_dimension=0, tiled=True
            ).astype(f32)

        def far_pack(self, *before):
            if before:
                self.arrived = [after(item, *before) for item in self.arrived]
            total = self.column().astype(bf16)
            self.blocks = [total[k * pair * share : (k + 1) * pair * share] for k in range(far_count)]
            self.packed = [
                self.block_of((far_index + step) % far_count) for step in range(1, far_count)
            ]
            return self.packed

        def block_of(self, index):
            result = self.blocks[0]
            for k in range(1, far_count):
                result = jnp.where(index == k, self.blocks[k], result)
            return result

        def far_send(self):
            self.arrived = [
                lax.ppermute(p, "ctx", far_shift(s + 1)) for s, p in enumerate(self.packed)
            ]

        def near_pack(self, *before):
            if before:
                self.arrived = [after(item, *before) for item in self.arrived]
            total = sum_of(self.block_of(far_index).astype(f32), self.arrived)
            low, high = total[:share], total[share:]
            self.own = jnp.where(is_high, high, low)
            self.packed = jnp.where(is_high, low, high).astype(bf16)
            return [self.packed]

        def near_send(self):
            self.got = lax.ppermute(self.packed, "ctx", near_swap).astype(f32)

        def finish_near(self):
            return jnp.concatenate(
                [
                    jnp.where(is_high, self.got, self.own),
                    jnp.where(is_high, self.own, self.got),
                ],
                axis=1,
            )

    def norm_back(values, gain, incoming):
        _, back = jax.vjp(rms_norm, values, gain)
        return back(incoming)

    d_feed_out, post_feed_part = norm_back(feed_out, feed_post, cot)
    d_feed_low = join_all(d_feed_out.astype(bf16))
    down_sum = Reduction(d_feed_low, mixed)
    down_sum.core_pack()
    down_sum.core_send()
    d_mixed = jnp.dot(
        after(d_feed_low, *down_sum.packed), down_mat, preferred_element_type=f32
    )
    _, gate_back = jax.vjp(gated_product, gate, upward)
    d_gate, d_upward = gate_back(d_mixed)
    d_gate = d_gate.astype(bf16)
    d_upward = d_upward.astype(bf16)

    down_sum.y_pack(d_gate, d_upward)
    down_sum.y_send()
    d_feed_part = contract(after(d_gate, *down_sum.packed), gate_mat, 1, 1) + contract(
        after(d_upward, *down_sum.packed), up_mat, 1, 1
    )
    packed = pack_all(d_feed_part)
    sent = send_all(packed)
    gate_sum = Reduction(after(feed_in, *packed), d_gate)
    gate_sum.core_pack()
    gate_sum.core_send()
    down_sum.far_pack(*gate_sum.packed)
    down_sum.far_send()
    up_sum = Reduction(after(feed_in, *down_sum.packed), d_upward)
    up_sum.core_pack()
    up_sum.core_send()
    gate_sum.y_pack(*up_sum.packed)
    gate_sum.y_send()
    own_feed = after(d_feed_part[:half], *gate_sum.packed)
    d_feed_in = sum_of(own_feed, sent)

    d_from_feed, pre_feed_part = norm_back(hidden_mid, feed_gain, d_feed_in)
    d_mid = cot + d_from_feed
    d_attend_out, post_attend_part = norm_back(attend_out, gain_out, d_mid)
    d_attend_own = d_attend_out.astype(bf16)
    d_attend_got = lax.ppermute(d_attend_own, "tensor", x_swap)
    up_sum.y_pack(d_attend_own)
    up_sum.y_send()
    d_attend_got = after(d_attend_got, *up_sum.packed)
    d_attend_low = jnp.concatenate([d_attend_own, d_attend_got], axis=0)
    d_attended = jnp.dot(d_attend_low, out_mat, preferred_element_type=f32).astype(bf16)
    out_sum = Reduction(after(d_attend_low, d_attended), attended)
    out_sum.core_pack()
    out_sum.core_send()
    gate_sum.far_pack(*out_sum.packed)
    gate_sum.far_send()
    d_attended = after(d_attended, *gate_sum.packed)
    d_query_pre, d_kv = attend_backward(
        queries,
        kv_all,
        d_attended,
        attended_wide,
        inverse_sums,
        cosine,
        sine,
        query_places,
        key_places,
        groups,
        per_group,
        ctx_count,
    )

    def slot(index, carried):
        block = d_kv[index * rows : (index + 1) * rows]
        if carried is not None:
            block = block + carried.astype(f32)
        return block.astype(bf16)

    def line_sum(step, left_block, right_block):
        right_pairs = [(i, i + 1) for i in range(0, step)]
        left_pairs = [(i, i - 1) for i in range(ctx_count - step, ctx_count)]
        return (
            lax.ppermute(left_block, "ctx", right_pairs),
            lax.ppermute(right_block, "ctx", left_pairs),
        )

    sent_blocks = (slot(1, None), slot(ctx_count - 1, None))
    carried = line_sum(1, *sent_blocks)
    out_sum.y_pack(*sent_blocks)
    out_sum.y_send()
    query_sum = Reduction(after(attend_in, *out_sum.packed), d_query_pre)
    query_sum.core_pack()
    query_sum.core_send()
    down_sum.near_pack(*query_sum.packed)
    down_sum.near_send()
    before = (*query_sum.packed, *out_sum.packed, down_sum.packed)
    for step in range(2, ctx_count):
        carried = [after(item, *before) for item in carried]
        sent_blocks = (slot(step, carried[0]), slot(ctx_count - step, carried[1]))
        carried = line_sum(step, *sent_blocks)
        before = ()
        if step == 2:
            query_sum.y_pack(*sent_blocks)
            query_sum.y_send()
            up_sum.far_pack(*query_sum.packed)
            up_sum.far_send()
            before = (*query_sum.packed, *up_sum.packed)
    query_part = contract(after(d_query_pre, *sent_blocks), query_mat, 1, 1)
    gate_sum.near_pack(query_part)
    gate_sum.near_send()
    carried = [after(item, query_part, gate_sum.packed) for item in carried]
    d_kv_local = sum_of(d_kv[:rows], carried)
    turned = []
    for g in range(groups):
        middle = (2 * g + 1) * HD
        turned += [
            turn(d_kv_local[:, middle - HD : middle], cosine, -sine),
            d_kv_local[:, middle : middle + HD],
        ]
    d_keyvalue = jnp.concatenate(turned, axis=1).astype(bf16)

    in_factor = lax.rsqrt(jnp.mean(inputs * inputs, axis=-1, keepdims=True) + epsilon)
    d_attend_part = query_part + contract(d_keyvalue, keyvalue_mat, 1, 1)
    pre_attend_part = jnp.sum(d_attend_part * inputs * in_factor, axis=0)
    gain_parts = jnp.stack([pre_attend_part, post_attend_part, pre_feed_part, post_feed_part])
    gain_parts = jnp.pad(gain_parts, ((0, pad_lanes - 4), (0, 0)))
    got = lax.ppermute(d_attend_part[half:].astype(bf16), "tensor", x_swap)

    keyvalue_sum = Reduction(attend_in, d_keyvalue, gain_parts)
    keyvalue_sum.core_pack()
    keyvalue_sum.core_send()
    keyvalue_sum.y_pack()
    keyvalue_sum.y_send()
    d_attend_in = d_attend_part[:half] + got.astype(f32)
    up_sum.near_pack(*keyvalue_sum.packed)
    up_sum.near_send()
    out_grad = out_sum.finish_ctx().T
    query_grad = query_sum.finish_ctx()
    attend_grad = keyvalue_sum.finish_ctx()
    down_grad = down_sum.finish_near().T
    gate_grad = gate_sum.finish_near()
    up_grad = up_sum.finish_near()
    key_grad = jnp.concatenate(
        [attend_grad[:, 2 * g * HD : (2 * g + 1) * HD] for g in range(groups)], axis=1
    )
    value_grad = jnp.concatenate(
        [attend_grad[:, (2 * g + 1) * HD : (2 * g + 2) * HD] for g in range(groups)], axis=1
    )
    gain_grads = attend_grad[:, keyvalue_width:]
    gain_grads = (gain_grads + lax.ppermute(gain_grads, "tensor", x_swap)).T

    d_from_attend, _ = norm_back(own_inputs, gain_in, d_attend_in)
    input_grad = join_absolute((d_mid + d_from_attend).astype(bf16)).astype(f32)[None]

    return (
        layer_output,
        input_grad,
        gain_grads[0],
        query_grad,
        key_grad,
        value_grad,
        out_grad,
        gain_grads[1],
        gain_grads[2],
        gate_grad,
        up_grad,
        down_grad,
        gain_grads[3],
    )


def solution(mesh):
    both = ("dp", "ctx")
    return jax.shard_map(
        body,
        mesh=mesh,
        in_specs=(
            P("dp", "ctx", None),
            P("dp", None),
            P(both),
            P(both, "tensor"),
            P(both, "tensor"),
            P(both, "tensor"),
            P("tensor", both),
            P(both),
            P(both),
            P(both, "tensor"),
            P(both, "tensor"),
            P("tensor", both),
            P(both),
            P("dp", "ctx", None),
        ),
        out_specs=(
            P("dp", "ctx", None),
            P("dp", "ctx", None),
            P(both),
            P(both, "tensor"),
            P(both, "tensor"),
            P(both, "tensor"),
            P("tensor", both),
            P(both),
            P(both),
            P(both, "tensor"),
            P(both, "tensor"),
            P("tensor", both),
            P(both),
        ),
        check_vma=False,
    )
```

```python
import functools

import jax
import jax.numpy as jnp
from jax import lax
from jax.experimental import pallas as pl
from jax.experimental.pallas import tpu as pltpu
from jax.sharding import PartitionSpec as P

HQ = 8
KV = 4
HD = 256
LEN = 2048

epsilon = 1e-06
cap_value = 50.0
gelu_coef = 0.7978845608028654
cores = 2
pad_lanes = 128

f32 = jnp.float32
bf16 = jnp.bfloat16


def rms_norm(values, gain):
    factor = lax.rsqrt(jnp.mean(values * values, axis=-1, keepdims=True) + epsilon)
    return values * factor * gain


def gelu_tanh(values):
    return (
        0.5 * values * (1.0 + jnp.tanh(gelu_coef * (values + 0.044715 * values * values * values)))
    )


def gated_product(gate, upward):
    return gelu_tanh(gate) * upward


def rotary_tables(positions, head_size):
    half = head_size // 2
    freqs = 10000.0 ** (-(jnp.arange(half, dtype=f32) * 2.0) / head_size)
    angle = positions.astype(f32)[:, None] * freqs[None, :]
    return (jnp.cos(angle), jnp.sin(angle))


attend_limit = 48 * 1024 * 1024


def dotted(left, right, left_dim, right_dim, precision=None):
    return lax.dot_general(
        left,
        right,
        (((left_dim,), (right_dim,)), ((), ())),
        precision=precision,
        preferred_element_type=f32,
    )


def turn(values, cosine, sine):
    half = HD // 2
    first, second = values[:, :half], values[:, half:]
    return jnp.concatenate(
        [first * cosine - second * sine, second * cosine + first * sine], axis=1
    )


def forward_kernel(chunks, pre_ref, kv_ref, cos_ref, sin_ref, qpos_ref, kpos_ref, q_ref, out_ref, low_ref, inv_ref):
    rows = pre_ref.shape[0]
    size = kv_ref.shape[0] // chunks
    q = turn(pre_ref[...], cos_ref[...], sin_ref[...]).astype(bf16)
    q_ref[...] = q
    qpos = qpos_ref[...]
    total = jnp.zeros((1, rows), f32)
    acc = jnp.zeros((HD, rows), f32)
    for c in range(chunks):
        part = pl.ds(c * size, size)
        raw = dotted(kv_ref[part, :HD], q, 1, 1)
        level = jnp.tanh(raw * (HD ** (-0.5) / cap_value))
        weight = jnp.where(qpos >= kpos_ref[part, :], jnp.exp(cap_value * level), 0.0)
        total = total + jnp.sum(weight, axis=0, keepdims=True)
        acc = acc + dotted(kv_ref[part, HD:], weight.astype(bf16), 0, 0)
    inverse = 1.0 / total
    inv_ref[0] = inverse
    out = (acc * inverse).T
    out_ref[...] = out
    low_ref[...] = out.astype(bf16)


def attend_forward(query_pre, kv_all, cosine, sine, qpos, kpos, groups, per_group, chunks):
    rows, width = query_pre.shape
    length = kv_all.shape[0]
    heads = groups * per_group
    by_head = pl.BlockSpec((rows, HD), lambda g, r: (0, g * per_group + r))
    fixed = lambda shape: pl.BlockSpec(shape, lambda g, r: (0, 0))
    return pl.pallas_call(
        functools.partial(forward_kernel, chunks),
        grid=(groups, per_group),
        in_specs=[
            by_head,
            pl.BlockSpec((length, 2 * HD), lambda g, r: (0, g)),
            fixed((rows, HD // 2)),
            fixed((rows, HD // 2)),
            fixed((1, rows)),
            fixed((length, 1)),
        ],
        out_specs=[
            by_head,
            by_head,
            by_head,
            pl.BlockSpec((1, 1, rows), lambda g, r: (g * per_group + r, 0, 0)),
        ],
        out_shape=[
            jax.ShapeDtypeStruct((rows, width), bf16),
            jax.ShapeDtypeStruct((rows, width), f32),
            jax.ShapeDtypeStruct((rows, width), bf16),
            jax.ShapeDtypeStruct((heads, 1, rows), f32),
        ],
        compiler_params=pltpu.CompilerParams(vmem_limit_bytes=attend_limit),
        cost_estimate=pl.CostEstimate(
            flops=rows * width,
            bytes_accessed=rows * width,
            transcendentals=0,
        ),
        name="attend_forward",
    )(query_pre, kv_all, cosine, sine, qpos, kpos)


def backward_kernel(per_group, q_ref, kv_ref, da_ref, out_ref, inv_ref, cos_ref, sin_ref, qpos_ref, kpos_ref, dq_ref, dkv_ref, delta_ref, sum_ref, both_ref):
    c, r = pl.program_id(1), pl.program_id(2)
    q, da = q_ref[...], da_ref[...]
    k, v = kv_ref[:, :HD], kv_ref[:, HD:]

    @pl.when(c == 0)
    def _():
        delta_ref[r] = dotted(
            jnp.ones((8, HD), f32), da.astype(f32) * out_ref[...], 1, 1, lax.Precision.HIGHEST
        )

    delta = delta_ref[r][0:1]
    level = jnp.tanh(dotted(k, q, 1, 1) * (HD ** (-0.5) / cap_value))
    seen = qpos_ref[...] >= kpos_ref[...]
    prob = jnp.where(seen, jnp.exp(cap_value * level), 0.0) * inv_ref[0]
    d_prob = dotted(v, da, 1, 1)
    d_raw = (prob * (d_prob - delta) * (1.0 - level * level)).astype(bf16)
    d_key = dotted(d_raw, q, 1, 0) * HD ** (-0.5)
    d_value = dotted(prob.astype(bf16), da, 1, 0)
    d_query = dotted(d_raw, k, 0, 0)

    @pl.when(r == 0)
    def _():
        both_ref[:, :HD] = d_key
        both_ref[:, HD:] = d_value

    @pl.when(r > 0)
    def _():
        both_ref[:, :HD] += d_key
        both_ref[:, HD:] += d_value

    @pl.when(r == per_group - 1)
    def _():
        dkv_ref[...] = both_ref[...].astype(bf16)

    @pl.when(c == 0)
    def _():
        sum_ref[r] = d_query

    @pl.when(c > 0)
    def _():
        sum_ref[r] += d_query

    for head in range(per_group):

        @pl.when((c == pl.num_programs(1) - 1) & (r == head))
        def _():
            whole = sum_ref[head] * HD ** (-0.5)
            dq_ref[:, head * HD : (head + 1) * HD] = turn(
                whole, cos_ref[...], -sin_ref[...]
            ).astype(bf16)


def attend_backward(queries, kv_all, d_attended, out, inverse, cosine, sine, qpos, kpos, groups, per_group, chunks):
    rows, width = queries.shape
    length = kv_all.shape[0]
    size = length // chunks
    heads = groups * per_group
    by_head = pl.BlockSpec((rows, HD), lambda g, c, r: (0, g * per_group + r))
    fixed = lambda shape: pl.BlockSpec(shape, lambda g, c, r: (0, 0))
    by_chunk = pl.BlockSpec((size, 2 * HD), lambda g, c, r: (c, g))
    return pl.pallas_call(
        functools.partial(backward_kernel, per_group),
        grid=(groups, chunks, per_group),
        in_specs=[
            by_head,
            by_chunk,
            by_head,
            by_head,
            pl.BlockSpec((1, 1, rows), lambda g, c, r: (g * per_group + r, 0, 0)),
            fixed((rows, HD // 2)),
            fixed((rows, HD // 2)),
            fixed((1, rows)),
            pl.BlockSpec((size, 1), lambda g, c, r: (c, 0)),
        ],
        out_specs=[
            pl.BlockSpec((rows, per_group * HD), lambda g, c, r: (0, g)),
            by_chunk,
        ],
        out_shape=[
            jax.ShapeDtypeStruct((rows, width), bf16),
            jax.ShapeDtypeStruct((length, groups * 2 * HD), bf16),
        ],
        scratch_shapes=[
            pltpu.VMEM((per_group, 8, rows), f32),
            pltpu.VMEM((per_group, rows, HD), f32),
            pltpu.VMEM((size, 2 * HD), f32),
        ],
        compiler_params=pltpu.CompilerParams(vmem_limit_bytes=attend_limit),
        cost_estimate=pl.CostEstimate(
            flops=rows * width,
            bytes_accessed=rows * width,
            transcendentals=0,
        ),
        name="attend_backward",
    )(queries, kv_all, d_attended, out, inverse, cosine, sine, qpos, kpos)


feed_limit = 56 * 1024 * 1024
feed_tile = 256


def feed_params():
    return dict(
        compiler_params=pltpu.CompilerParams(vmem_limit_bytes=feed_limit),
        cost_estimate=pl.CostEstimate(flops=1000000, bytes_accessed=1000000, transcendentals=0),
    )


def whole_block(array):
    return pl.BlockSpec(array.shape, lambda n: (0, 0))


def column_tile(array):
    return pl.BlockSpec((array.shape[0], feed_tile), lambda n: (0, n))


def row_tile(array):
    return pl.BlockSpec((feed_tile, array.shape[1]), lambda n: (n, 0))


def mix_kernel(x_ref, gate_mat_ref, up_mat_ref, gate_ref, up_ref, mixed_ref):
    x = x_ref[...]
    gate = dotted(x, gate_mat_ref[...], 1, 0)
    upward = dotted(x, up_mat_ref[...], 1, 0)
    gate_ref[...] = gate
    up_ref[...] = upward
    inner = gelu_coef * (gate + 0.044715 * gate * gate * gate)
    mixed_ref[...] = (0.5 * gate * (1.0 + jnp.tanh(inner)) * upward).astype(bf16)


def mix_forward(x, gate_mat, up_mat):
    rows, hidden = x.shape[0], gate_mat.shape[1]
    shapes = [jax.ShapeDtypeStruct((rows, hidden), kind) for kind in (f32, f32, bf16)]
    return pl.pallas_call(
        mix_kernel,
        grid=(hidden // feed_tile,),
        in_specs=[whole_block(x), column_tile(gate_mat), column_tile(up_mat)],
        out_specs=[column_tile(shape) for shape in shapes],
        out_shape=shapes,
        name="mix_forward",
        **feed_params(),
    )(x, gate_mat, up_mat)


def mix_back_kernel(d_ref, down_mat_ref, gate_ref, up_ref, d_gate_ref, d_up_ref):
    d_mixed = dotted(d_ref[...], down_mat_ref[...], 1, 0)
    gate = gate_ref[...]
    square = gate * gate
    level = jnp.tanh(gelu_coef * gate * (1.0 + 0.044715 * square))
    slope = gelu_coef * (1.0 + 3.0 * 0.044715 * square)
    curve = 0.5 * (1.0 + level)
    d_curve = curve + 0.5 * gate * (1.0 - level * level) * slope
    d_gate_ref[...] = (d_mixed * up_ref[...] * d_curve).astype(bf16)
    d_up_ref[...] = (d_mixed * (gate * curve)).astype(bf16)


def mix_backward(d_out, down_mat, gate, upward):
    shapes = [jax.ShapeDtypeStruct(gate.shape, bf16)] * 2
    return pl.pallas_call(
        mix_back_kernel,
        grid=(gate.shape[1] // feed_tile,),
        in_specs=[
            whole_block(d_out),
            column_tile(down_mat),
            column_tile(gate),
            column_tile(upward),
        ],
        out_specs=[column_tile(shape) for shape in shapes],
        out_shape=shapes,
        name="mix_backward",
        **feed_params(),
    )(d_out, down_mat, gate, upward)


def spread_kernel(count, half, *refs):
    lefts, rights, outs = refs[:count], refs[count : 2 * count], refs[2 * count :]
    total = dotted(lefts[0][...], rights[0][...], 1, 1)
    for left, right in zip(lefts[1:], rights[1:]):
        total = total + dotted(left[...], right[...], 1, 1)
    for k, out in enumerate(outs):
        out[...] = total[k * half : (k + 1) * half].astype(out.dtype)


def product_blocks(lefts, rights, half):
    rows, width = lefts[0].shape[0], rights[0].shape[0]
    shapes = [
        jax.ShapeDtypeStruct((half, width), bf16 if k else f32) for k in range(rows // half)
    ]
    return pl.pallas_call(
        functools.partial(spread_kernel, len(lefts), half),
        grid=(width // feed_tile,),
        in_specs=[whole_block(left) for left in lefts] + [row_tile(right) for right in rights],
        out_specs=[column_tile(shape) for shape in shapes],
        out_shape=shapes,
        name="product_blocks",
        **feed_params(),
    )(*lefts, *rights)


def contract(left, right, left_dim, right_dim):
    return lax.dot_general(
        left, right, (((left_dim,), (right_dim,)), ((), ())), preferred_element_type=f32
    )


def body(
    layer_input,
    block_order,
    pre_attend,
    query_weight,
    key_weight,
    value_weight,
    output_weight,
    post_attend,
    pre_feed,
    gate_weight,
    up_weight,
    down_weight,
    post_feed,
    cotangent,
):
    _, rows, width = layer_input.shape
    block_len = LEN // block_order.shape[1]
    per_group = HQ // KV
    tensor_count = lax.axis_size("tensor")
    groups = KV // tensor_count
    factor = HD ** (-0.5)
    dp_count = lax.axis_size(("y", "core"))
    ctx_count = lax.axis_size("ctx")
    tensor_index = lax.axis_index("tensor")
    ctx_index = lax.axis_index("ctx")
    dp_index = lax.axis_index(("y", "core"))
    y_count = dp_count // cores
    y_index = dp_index // cores
    core_index = dp_index % cores
    dp_axes = ("y", "core")
    share = width // (dp_count * ctx_count)
    quarter = share * ctx_count
    half = rows // tensor_count
    pair = 2
    far_count = ctx_count // pair
    far_index = ctx_index // pair
    near_index = ctx_index % pair
    x_swap = [(0, 1), (1, 0)]
    all_swaps = {}
    for bz, bx in ((0, 1), (1, 0), (1, 1)):
        all_swaps[bz, bx] = [
            (c * 2 + t, (c ^ bz) * 2 + (t ^ bx)) for c in range(ctx_count) for t in range(2)
        ]
    near_swap = [(c, c ^ 1) for c in range(ctx_count)]

    def far_shift(step):
        return [
            (c, ((c // pair + step) % far_count) * pair + c % pair) for c in range(ctx_count)
        ]

    def along(dy, dc):
        pairs = []
        for y in range(y_count):
            for core in range(cores):
                target = ((y + dy) % y_count) * cores + (core + dc) % cores
                pairs.append((y * cores + core, target))
        return pairs

    def after(value, *others):
        return lax.optimization_barrier((value, *others))[0]

    def chosen(parts, index, place):
        count = len(parts)
        result = parts[0]
        for step in range(1, count):
            result = jnp.where((index - place) % count == step, parts[step], result)
        return result

    def in_order(parts, index):
        return jnp.concatenate([chosen(parts, index, k) for k in range(len(parts))], axis=0)

    def relative(values):
        first, second = values[:half], values[half:]
        flip = tensor_index == 1
        return jnp.concatenate(
            [jnp.where(flip, second, first), jnp.where(flip, first, second)], axis=0
        )

    def join(own):
        return jnp.concatenate([own, lax.ppermute(own, "tensor", x_swap)], axis=0)

    def join_absolute(own):
        return relative(join(own))

    def join_all(own):
        parts = [own]
        for pairs in all_swaps.values():
            parts.append(lax.ppermute(own, ("ctx", "tensor"), pairs))
        return jnp.concatenate(parts, axis=0)

    def pack_all(product):
        return [product[(k + 1) * half : (k + 2) * half].astype(bf16) for k in range(3)]

    def send_all(parts):
        return [
            lax.ppermute(part, ("ctx", "tensor"), pairs)
            for part, pairs in zip(parts, all_swaps.values())
        ]

    def sum_of(own, parts):
        for item in parts:
            own = own + item.astype(f32)
        return own

    all_pos = (
        block_order[0][:, None] * block_len + jnp.arange(block_len, dtype=jnp.int32)[None, :]
    ).reshape(ctx_count, tensor_count, half)
    all_pos = jnp.where(tensor_index == 1, all_pos[:, ::-1], all_pos).reshape(ctx_count, rows)
    local_pos = lax.dynamic_slice_in_dim(all_pos, ctx_index, 1, 0)[0]
    cosine, sine = rotary_tables(local_pos, HD)
    query_places = local_pos[None, :]
    key_places = all_pos.reshape(LEN, 1)

    both = ("y", "core", "ctx")
    gain_pack = jnp.stack([pre_attend, post_attend, pre_feed, post_feed], axis=1)
    gain_pack = jnp.pad(gain_pack, ((0, 0), (0, pad_lanes - 4)))
    heads_in_turn = []
    for g in range(groups):
        heads_in_turn += [
            key_weight[:, g * HD : (g + 1) * HD],
            value_weight[:, g * HD : (g + 1) * HD],
        ]
    keyvalue_pack = jnp.concatenate([*heads_in_turn, gain_pack], axis=1)
    keyvalue_all = lax.all_gather(keyvalue_pack, both, axis=0, tiled=True)
    query_mat = lax.all_gather(query_weight, both, axis=0, tiled=True)
    out_mat = lax.all_gather(output_weight.T, both, axis=0, tiled=True)

    hidden = gate_weight.shape[1] // pair
    is_high = near_index == 1

    def split(weight):
        low, high = weight[:, :hidden], weight[:, hidden:]
        return jnp.where(is_high, high, low), jnp.where(is_high, low, high)

    def far_pack(mine, got):
        return jnp.concatenate(
            [jnp.where(is_high, got, mine), jnp.where(is_high, mine, got)], axis=0
        )

    def far_start(block):
        return [lax.ppermute(block, "ctx", far_shift(s)) for s in range(1, far_count)]

    gate_mine, gate_other = split(gate_weight)
    up_mine, up_other = split(up_weight)
    down_mine, down_other = split(down_weight.T)
    gate_got = lax.ppermute(gate_other, "ctx", near_swap)
    rest_got = lax.ppermute(jnp.concatenate([up_other, down_other], axis=0), "ctx", near_swap)
    gate_block = far_pack(gate_mine, gate_got)
    gate_far = far_start(gate_block)
    up_block = far_pack(up_mine, rest_got[: rest_got.shape[0] // 2])
    down_block = far_pack(down_mine, rest_got[rest_got.shape[0] // 2 :])

    query_width = query_weight.shape[1]
    keyvalue_width = 2 * key_weight.shape[1]
    keyvalue_all = after(keyvalue_all, up_block, down_block)
    keyvalue_mat = keyvalue_all[:, :keyvalue_width]
    gains = keyvalue_all[:, keyvalue_width : keyvalue_width + 8].T.astype(f32)
    gain_in, gain_out, feed_gain, feed_post = gains[0], gains[1], gains[2], gains[3]

    inputs = relative(layer_input[0].astype(f32))
    own_inputs = inputs[:half]
    cot = lax.dynamic_slice_in_dim(cotangent[0], tensor_index * half, half, 0).astype(f32)

    attend_in = rms_norm(inputs, gain_in).astype(bf16)
    keyvalue_pre = jnp.dot(attend_in, keyvalue_mat, preferred_element_type=f32)
    turned = []
    for g in range(groups):
        middle = (2 * g + 1) * HD
        turned += [
            turn(keyvalue_pre[:, middle - HD : middle], cosine, sine),
            keyvalue_pre[:, middle : middle + HD],
        ]
    kv_local = jnp.concatenate(turned, axis=1).astype(bf16)

    from_left, from_right = [kv_local], [kv_local]

    def line_step(step, left_block, right_block):
        right_pairs = [(i, i + 1) for i in range(step - 1, ctx_count - 1)]
        left_pairs = [(i, i - 1) for i in range(1, ctx_count - step + 1)]
        from_left.append(lax.ppermute(left_block, "ctx", right_pairs))
        from_right.append(lax.ppermute(right_block, "ctx", left_pairs))

    line_step(1, kv_local, kv_local)
    gate_far = [after(part, kv_local) for part in gate_far]
    gate_rows = in_order([gate_block] + gate_far, far_index)
    gate_mat = lax.all_gather(gate_rows, dp_axes, axis=0, tiled=True)
    up_far = far_start(after(up_block, gate_rows))
    for step in range(2, ctx_count):
        left_block, right_block = from_left[-1], from_right[-1]
        if step == 2:
            left_block, right_block = after(left_block, gate_rows), after(right_block, gate_rows)
        line_step(step, left_block, right_block)
    last_blocks = (from_left[-2], from_right[-2])
    query_pre = jnp.dot(
        after(attend_in, *last_blocks), query_mat, preferred_element_type=f32
    )
    kv_parts = [kv_local]
    for step in range(1, ctx_count):
        kv_parts.append(
            jnp.where(ctx_index >= step, from_left[step], from_right[ctx_count - step])
        )
    kv_all = in_order(kv_parts, ctx_index)
    up_far = [after(part, *last_blocks) for part in up_far]
    up_rows = in_order([up_block] + up_far, far_index)
    up_mat = lax.all_gather(up_rows, dp_axes, axis=0, tiled=True)
    down_far = far_start(after(down_block, up_rows))
    kv_all = after(kv_all, up_rows)
    queries, attended_wide, attended, inverse_sums = attend_forward(
        query_pre, kv_all, cosine, sine, query_places, key_places, groups, per_group, ctx_count
    )
    other = contract(attended[half:], out_mat, 1, 1).astype(bf16)
    got = lax.ppermute(other, "tensor", x_swap)
    down_far = [after(part, got) for part in down_far]
    down_rows = in_order([down_block] + down_far, far_index)
    down_mat = lax.all_gather(down_rows, dp_axes, axis=0, tiled=True)
    attend_out = contract(attended[:half], out_mat, 1, 1) + got.astype(f32)
    hidden_mid = own_inputs + rms_norm(attend_out, gain_out)
    feed_own = rms_norm(hidden_mid, feed_gain).astype(bf16)
    feed_in = join_all(feed_own)
    gate, upward, mixed = mix_forward(feed_in, gate_mat, up_mat)
    feed_own, *sent = product_blocks([mixed], [down_mat], half)
    sent = send_all(sent)
    feed_out = sum_of(feed_own, sent)
    layer_output = join_absolute(
        (hidden_mid + rms_norm(feed_out, feed_post)).astype(bf16)
    )[None]

    class Reduction:
        def __init__(self, left, right):
            self.whole = contract(left, right, 0, 0).astype(bf16)

        def piece(self, dy, dc):
            index = ((y_index + dy) % y_count) * cores + (core_index + dc) % cores
            return lax.dynamic_slice_in_dim(self.whole, index * quarter, quarter, 0)

        def core_pack(self):
            self.packed = [self.piece(dy, 1) for dy in range(y_count)]
            return self.packed

        def core_send(self):
            self.swapped = [lax.ppermute(p, dp_axes, along(0, 1)) for p in self.packed]

        def y_pack(self, *before):
            swapped = self.swapped
            if before:
                swapped = [after(item, *before) for item in swapped]
            self.packed = [
                (self.piece(dy, 0).astype(f32) + swapped[dy].astype(f32)).astype(bf16)
                for dy in range(1, y_count)
            ]
            return self.packed

        def y_send(self):
            self.arrived = [
                lax.ppermute(p, dp_axes, along(dy + 1, 0)) for dy, p in enumerate(self.packed)
            ]

        def sum_y(self, *before):
            arrived = self.arrived
            if before:
                arrived = [after(item, *before) for item in arrived]
            total = self.piece(0, 0).astype(f32) + self.swapped[0].astype(f32)
            self.total = sum_of(total, arrived).astype(bf16)
            return self.total

        def finish_ctx(self):
            return lax.psum_scatter(
                self.total, "ctx", scatter_dimension=0, tiled=True
            ).astype(f32)

        def block_of(self, index):
            result = self.blocks[0]
            for k in range(1, far_count):
                result = jnp.where(index == k, self.blocks[k], result)
            return result

        def far_pack(self, *before):
            total = self.sum_y(*before)
            self.blocks = [
                total[k * pair * share : (k + 1) * pair * share] for k in range(far_count)
            ]
            self.packed = [
                self.block_of((far_index + step) % far_count) for step in range(1, far_count)
            ]
            return self.packed

        def far_send(self):
            self.arrived = [
                lax.ppermute(p, "ctx", far_shift(s + 1)) for s, p in enumerate(self.packed)
            ]

        def near_pack(self, *before):
            arrived = self.arrived
            if before:
                arrived = [after(item, *before) for item in arrived]
            total = sum_of(self.block_of(far_index).astype(f32), arrived)
            low, high = total[:share], total[share:]
            self.own = jnp.where(is_high, high, low)
            self.other = jnp.where(is_high, low, high).astype(bf16)
            return self.other

    def near_send(*sums):
        sent = sums[0].other
        if len(sums) > 1:
            sent = jnp.concatenate([item.other for item in sums], axis=0)
        got = lax.ppermute(sent, "ctx", near_swap).astype(f32)
        for k, item in enumerate(sums):
            item.got = got[k * share : (k + 1) * share]

    def finish_near(own, got):
        return jnp.concatenate(
            [jnp.where(is_high, got, own), jnp.where(is_high, own, got)], axis=1
        )

    def norm_back(values, gain, incoming):
        _, back = jax.vjp(rms_norm, values, gain)
        return back(incoming)

    d_feed_out, post_feed_part = norm_back(feed_out, feed_post, cot)
    d_feed_low = join_all(d_feed_out.astype(bf16))
    down_sum = Reduction(d_feed_low, mixed)
    down_sum.core_pack()
    down_sum.core_send()
    down_sum.y_pack()
    down_sum.y_send()
    d_feed_tied = after(d_feed_low, *down_sum.packed)
    d_gate, d_upward = mix_backward(d_feed_tied, down_mat, gate, upward)
    d_tied = (after(d_gate, *down_sum.packed), after(d_upward, *down_sum.packed))
    d_feed_own, *packed = product_blocks(d_tied, [gate_mat, up_mat], half)
    sent = send_all(packed)
    gate_sum = Reduction(after(feed_in, *packed), d_gate)
    gate_sum.core_pack()
    gate_sum.core_send()
    down_sum.far_pack(*gate_sum.packed)
    down_sum.far_send()
    up_sum = Reduction(after(feed_in, *down_sum.packed), d_upward)
    up_sum.core_pack()
    up_sum.core_send()
    gate_sum.y_pack(*up_sum.packed)
    gate_sum.y_send()
    own_feed = after(d_feed_own, *up_sum.packed, *gate_sum.packed)
    d_feed_in = sum_of(own_feed, sent)

    d_from_feed, pre_feed_part = norm_back(hidden_mid, feed_gain, d_feed_in)
    d_mid = cot + d_from_feed
    d_attend_out, post_attend_part = norm_back(attend_out, gain_out, d_mid)
    d_attend_own = d_attend_out.astype(bf16)
    d_attend_got = lax.ppermute(d_attend_own, "tensor", x_swap)
    up_sum.y_pack(d_attend_own)
    up_sum.y_send()
    d_attend_got = after(d_attend_got, *up_sum.packed)
    d_attend_low = jnp.concatenate([d_attend_own, d_attend_got], axis=0)
    d_attended = jnp.dot(d_attend_low, out_mat, preferred_element_type=f32).astype(bf16)
    out_sum = Reduction(after(d_attend_low, d_attended), attended)
    out_sum.core_pack()
    out_sum.core_send()
    gate_sum.far_pack(*out_sum.packed)
    gate_sum.far_send()
    d_attended = after(d_attended, *gate_sum.packed)
    d_attended = after(d_attended, *down_sum.arrived)
    d_query_pre, d_kv = attend_backward(
        queries,
        kv_all,
        d_attended,
        attended_wide,
        inverse_sums,
        cosine,
        sine,
        query_places,
        key_places,
        groups,
        per_group,
        ctx_count,
    )
    d_kv = after(d_kv, *gate_sum.arrived)
    d_kv_local = lax.psum_scatter(d_kv, "ctx", scatter_dimension=0, tiled=True).astype(f32)
    out_sum.y_pack(d_kv)
    out_sum.y_send()
    query_sum = Reduction(after(attend_in, *out_sum.packed), d_query_pre)
    query_sum.core_pack()
    query_sum.core_send()
    last = query_sum.packed
    down_sum.near_pack(*query_sum.packed)
    near_send(down_sum)
    last = [down_sum.other]
    up_sum.far_pack(*last)
    up_sum.far_send()
    query_sum.y_pack(*up_sum.packed)
    query_sum.y_send()
    query_part = contract(after(d_query_pre, *query_sum.packed), query_mat, 1, 1)
    last = [query_part]
    gate_sum.near_pack(*last)
    near_send(gate_sum)
    last = [gate_sum.other]
    out_sum.sum_y(*last)
    d_kv_local = after(d_kv_local, out_sum.total)
    turned = []
    for g in range(groups):
        middle = (2 * g + 1) * HD
        turned += [
            turn(d_kv_local[:, middle - HD : middle], cosine, -sine),
            d_kv_local[:, middle : middle + HD],
        ]
    d_keyvalue = jnp.concatenate(turned, axis=1).astype(bf16)

    keyvalue_sum = Reduction(attend_in, d_keyvalue)
    keyvalue_sum.core_pack()
    keyvalue_sum.core_send()
    keyvalue_part = contract(
        after(d_keyvalue, *keyvalue_sum.packed), keyvalue_mat, 1, 1
    )
    d_attend_part = query_part + keyvalue_part
    d_attend_sent = d_attend_part[half:].astype(bf16)
    got = lax.ppermute(d_attend_sent, "tensor", x_swap)
    keyvalue_sum.y_pack(d_attend_sent)
    keyvalue_sum.y_send()
    query_sum.sum_y(d_keyvalue)
    up_sum.near_pack(*keyvalue_sum.packed)
    near_send(up_sum)
    keyvalue_sum.sum_y()
    out_grad = out_sum.finish_ctx().T
    query_grad = query_sum.finish_ctx()
    attend_grad = keyvalue_sum.finish_ctx()

    in_factor = lax.rsqrt(jnp.mean(inputs * inputs, axis=-1, keepdims=True) + epsilon)
    pre_attend_part = jnp.sum(
        after(d_attend_part, *keyvalue_sum.packed) * inputs * in_factor, axis=0
    )
    gain_grads = jnp.stack([pre_attend_part, post_attend_part, pre_feed_part, post_feed_part])

    def swap_sum(values, axis, count):
        bit = 1
        while bit < count:
            pairs = [(i, i ^ bit) for i in range(count)]
            values = values + lax.ppermute(values, axis, pairs)
            bit *= 2
        return values

    gain_grads = swap_sum(gain_grads, dp_axes, dp_count)
    gain_grads = swap_sum(gain_grads, "ctx", ctx_count)
    gain_grads = swap_sum(gain_grads, "tensor", tensor_count)
    place = dp_index * ctx_count + ctx_index
    gain_grads = gain_grads.reshape(4, dp_count * ctx_count, share)
    gain_grads = lax.dynamic_slice_in_dim(gain_grads, place, 1, 1)[:, 0]

    down_grad = finish_near(down_sum.own, down_sum.got).T
    gate_grad = finish_near(gate_sum.own, gate_sum.got)
    up_grad = finish_near(up_sum.own, up_sum.got)
    key_grad = jnp.concatenate(
        [attend_grad[:, 2 * g * HD : (2 * g + 1) * HD] for g in range(groups)], axis=1
    )
    value_grad = jnp.concatenate(
        [attend_grad[:, (2 * g + 1) * HD : (2 * g + 2) * HD] for g in range(groups)], axis=1
    )

    d_attend_in = after(d_attend_part[:half], *keyvalue_sum.packed) + got.astype(f32)
    d_from_attend, _ = norm_back(own_inputs, gain_in, d_attend_in)
    input_grad = join_absolute((d_mid + d_from_attend).astype(bf16)).astype(f32)[None]

    return (
        layer_output,
        input_grad,
        gain_grads[0],
        query_grad,
        key_grad,
        value_grad,
        out_grad,
        gain_grads[1],
        gain_grads[2],
        gate_grad,
        up_grad,
        down_grad,
        gain_grads[3],
    )


def solution(mesh):
    dp_count, ctx_count, tensor_count = mesh.devices.shape
    mesh = jax.sharding.Mesh(
        mesh.devices.reshape(dp_count // cores, cores, ctx_count, tensor_count),
        ("y", "core", "ctx", "tensor"),
    )
    dp = ("y", "core")
    both = ("y", "core", "ctx")
    return jax.shard_map(
        body,
        mesh=mesh,
        in_specs=(
            P(dp, "ctx", None),
            P(dp, None),
            P(both),
            P(both, "tensor"),
            P(both, "tensor"),
            P(both, "tensor"),
            P("tensor", both),
            P(both),
            P(both),
            P(both, "tensor"),
            P(both, "tensor"),
            P("tensor", both),
            P(both),
            P(dp, "ctx", None),
        ),
        out_specs=(
            P(dp, "ctx", None),
            P(dp, "ctx", None),
            P(both),
            P(both, "tensor"),
            P(both, "tensor"),
            P(both, "tensor"),
            P("tensor", both),
            P(both),
            P(both),
            P(both, "tensor"),
            P(both, "tensor"),
            P("tensor", both),
            P(both),
        ),
        check_vma=False,
    )
```

```python
import functools

import jax
import jax.numpy as jnp
from jax import lax
from jax.experimental import pallas as pl
from jax.experimental.pallas import tpu as pltpu
from jax.sharding import PartitionSpec as P

HQ = 8
KV = 4
HD = 256
LEN = 2048

epsilon = 1e-06
cap_value = 50.0
gelu_coef = 0.7978845608028654
cores = 2
pad_lanes = 128

f32 = jnp.float32
bf16 = jnp.bfloat16


def rms_norm(values, gain):
    factor = lax.rsqrt(jnp.mean(values * values, axis=-1, keepdims=True) + epsilon)
    return values * factor * gain


def gelu_tanh(values):
    return (
        0.5 * values * (1.0 + jnp.tanh(gelu_coef * (values + 0.044715 * values * values * values)))
    )


def gated_product(gate, upward):
    return gelu_tanh(gate) * upward


def rotary_tables(positions, head_size):
    half = head_size // 2
    freqs = 10000.0 ** (-(jnp.arange(half, dtype=f32) * 2.0) / head_size)
    angle = positions.astype(f32)[:, None] * freqs[None, :]
    return (jnp.cos(angle), jnp.sin(angle))


attend_limit = 48 * 1024 * 1024


def dotted(left, right, left_dim, right_dim, precision=None):
    return lax.dot_general(
        left,
        right,
        (((left_dim,), (right_dim,)), ((), ())),
        precision=precision,
        preferred_element_type=f32,
    )


def turn(values, cosine, sine):
    half = HD // 2
    first, second = values[:, :half], values[:, half:]
    return jnp.concatenate(
        [first * cosine - second * sine, second * cosine + first * sine], axis=1
    )


def forward_kernel(chunks, pre_ref, kv_ref, cos_ref, sin_ref, qpos_ref, kpos_ref, q_ref, out_ref, low_ref, inv_ref):
    rows = pre_ref.shape[0]
    size = kv_ref.shape[0] // chunks
    q = turn(pre_ref[...], cos_ref[...], sin_ref[...]).astype(bf16)
    q_ref[...] = q
    qpos = qpos_ref[...]
    total = jnp.zeros((1, rows), f32)
    acc = jnp.zeros((HD, rows), f32)
    for c in range(chunks):
        part = pl.ds(c * size, size)
        raw = dotted(kv_ref[part, :HD], q, 1, 1)
        level = jnp.tanh(raw * (HD ** (-0.5) / cap_value))
        weight = jnp.where(qpos >= kpos_ref[part, :], jnp.exp(cap_value * level), 0.0)
        total = total + jnp.sum(weight, axis=0, keepdims=True)
        acc = acc + dotted(kv_ref[part, HD:], weight.astype(bf16), 0, 0)
    inverse = 1.0 / total
    inv_ref[0] = inverse
    out = (acc * inverse).T
    out_ref[...] = out
    low_ref[...] = out.astype(bf16)


def attend_forward(query_pre, kv_all, cosine, sine, qpos, kpos, groups, per_group, chunks):
    rows, width = query_pre.shape
    length = kv_all.shape[0]
    heads = groups * per_group
    by_head = pl.BlockSpec((rows, HD), lambda g, r: (0, g * per_group + r))
    fixed = lambda shape: pl.BlockSpec(shape, lambda g, r: (0, 0))
    return pl.pallas_call(
        functools.partial(forward_kernel, chunks),
        grid=(groups, per_group),
        in_specs=[
            by_head,
            pl.BlockSpec((length, 2 * HD), lambda g, r: (0, g)),
            fixed((rows, HD // 2)),
            fixed((rows, HD // 2)),
            fixed((1, rows)),
            fixed((length, 1)),
        ],
        out_specs=[
            by_head,
            by_head,
            by_head,
            pl.BlockSpec((1, 1, rows), lambda g, r: (g * per_group + r, 0, 0)),
        ],
        out_shape=[
            jax.ShapeDtypeStruct((rows, width), bf16),
            jax.ShapeDtypeStruct((rows, width), f32),
            jax.ShapeDtypeStruct((rows, width), bf16),
            jax.ShapeDtypeStruct((heads, 1, rows), f32),
        ],
        compiler_params=pltpu.CompilerParams(vmem_limit_bytes=attend_limit),
        cost_estimate=pl.CostEstimate(
            flops=rows * width,
            bytes_accessed=rows * width,
            transcendentals=0,
        ),
        name="attend_forward",
    )(query_pre, kv_all, cosine, sine, qpos, kpos)


def backward_kernel(per_group, q_ref, kv_ref, da_ref, out_ref, inv_ref, cos_ref, sin_ref, qpos_ref, kpos_ref, dq_ref, dkv_ref, delta_ref, sum_ref, both_ref):
    c, r = pl.program_id(1), pl.program_id(2)
    q, da = q_ref[...], da_ref[...]
    k, v = kv_ref[:, :HD], kv_ref[:, HD:]

    @pl.when(c == 0)
    def _():
        delta_ref[r] = dotted(
            jnp.ones((8, HD), f32), da.astype(f32) * out_ref[...], 1, 1, lax.Precision.HIGHEST
        )

    delta = delta_ref[r][0:1]
    level = jnp.tanh(dotted(k, q, 1, 1) * (HD ** (-0.5) / cap_value))
    seen = qpos_ref[...] >= kpos_ref[...]
    prob = jnp.where(seen, jnp.exp(cap_value * level), 0.0) * inv_ref[0]
    d_prob = dotted(v, da, 1, 1)
    d_raw = (prob * (d_prob - delta) * (1.0 - level * level)).astype(bf16)
    d_key = dotted(d_raw, q, 1, 0) * HD ** (-0.5)
    d_value = dotted(prob.astype(bf16), da, 1, 0)
    d_query = dotted(d_raw, k, 0, 0)

    @pl.when(r == 0)
    def _():
        both_ref[:, :HD] = d_key
        both_ref[:, HD:] = d_value

    @pl.when(r > 0)
    def _():
        both_ref[:, :HD] += d_key
        both_ref[:, HD:] += d_value

    @pl.when(r == per_group - 1)
    def _():
        dkv_ref[...] = both_ref[...].astype(bf16)

    @pl.when(c == 0)
    def _():
        sum_ref[r] = d_query

    @pl.when(c > 0)
    def _():
        sum_ref[r] += d_query

    for head in range(per_group):

        @pl.when((c == pl.num_programs(1) - 1) & (r == head))
        def _():
            whole = sum_ref[head] * HD ** (-0.5)
            dq_ref[:, head * HD : (head + 1) * HD] = turn(
                whole, cos_ref[...], -sin_ref[...]
            ).astype(bf16)


def attend_backward(queries, kv_all, d_attended, out, inverse, cosine, sine, qpos, kpos, groups, per_group, chunks):
    rows, width = queries.shape
    length = kv_all.shape[0]
    size = length // chunks
    heads = groups * per_group
    by_head = pl.BlockSpec((rows, HD), lambda g, c, r: (0, g * per_group + r))
    fixed = lambda shape: pl.BlockSpec(shape, lambda g, c, r: (0, 0))
    by_chunk = pl.BlockSpec((size, 2 * HD), lambda g, c, r: (c, g))
    return pl.pallas_call(
        functools.partial(backward_kernel, per_group),
        grid=(groups, chunks, per_group),
        in_specs=[
            by_head,
            by_chunk,
            by_head,
            by_head,
            pl.BlockSpec((1, 1, rows), lambda g, c, r: (g * per_group + r, 0, 0)),
            fixed((rows, HD // 2)),
            fixed((rows, HD // 2)),
            fixed((1, rows)),
            pl.BlockSpec((size, 1), lambda g, c, r: (c, 0)),
        ],
        out_specs=[
            pl.BlockSpec((rows, per_group * HD), lambda g, c, r: (0, g)),
            by_chunk,
        ],
        out_shape=[
            jax.ShapeDtypeStruct((rows, width), bf16),
            jax.ShapeDtypeStruct((length, groups * 2 * HD), bf16),
        ],
        scratch_shapes=[
            pltpu.VMEM((per_group, 8, rows), f32),
            pltpu.VMEM((per_group, rows, HD), f32),
            pltpu.VMEM((size, 2 * HD), f32),
        ],
        compiler_params=pltpu.CompilerParams(vmem_limit_bytes=attend_limit),
        cost_estimate=pl.CostEstimate(
            flops=rows * width,
            bytes_accessed=rows * width,
            transcendentals=0,
        ),
        name="attend_backward",
    )(queries, kv_all, d_attended, out, inverse, cosine, sine, qpos, kpos)


feed_limit = 56 * 1024 * 1024
feed_tile = 256


def feed_params():
    return dict(
        compiler_params=pltpu.CompilerParams(vmem_limit_bytes=feed_limit),
        cost_estimate=pl.CostEstimate(flops=1000000, bytes_accessed=1000000, transcendentals=0),
    )


def whole_block(array):
    return pl.BlockSpec(array.shape, lambda n: (0, 0))


def column_tile(array):
    return pl.BlockSpec((array.shape[0], feed_tile), lambda n: (0, n))


def row_tile(array):
    return pl.BlockSpec((feed_tile, array.shape[1]), lambda n: (n, 0))


def mix_kernel(x_ref, gate_mat_ref, up_mat_ref, gate_ref, up_ref, mixed_ref):
    x = x_ref[...]
    gate = dotted(x, gate_mat_ref[...], 1, 0)
    upward = dotted(x, up_mat_ref[...], 1, 0)
    gate_ref[...] = gate
    up_ref[...] = upward
    inner = gelu_coef * (gate + 0.044715 * gate * gate * gate)
    mixed_ref[...] = (0.5 * gate * (1.0 + jnp.tanh(inner)) * upward).astype(bf16)


def mix_forward(x, gate_mat, up_mat):
    rows, hidden = x.shape[0], gate_mat.shape[1]
    shapes = [jax.ShapeDtypeStruct((rows, hidden), kind) for kind in (f32, f32, bf16)]
    return pl.pallas_call(
        mix_kernel,
        grid=(hidden // feed_tile,),
        in_specs=[whole_block(x), column_tile(gate_mat), column_tile(up_mat)],
        out_specs=[column_tile(shape) for shape in shapes],
        out_shape=shapes,
        name="mix_forward",
        **feed_params(),
    )(x, gate_mat, up_mat)


def mix_back_kernel(d_ref, down_mat_ref, gate_ref, up_ref, d_gate_ref, d_up_ref):
    d_mixed = dotted(d_ref[...], down_mat_ref[...], 1, 0)
    gate = gate_ref[...]
    square = gate * gate
    level = jnp.tanh(gelu_coef * gate * (1.0 + 0.044715 * square))
    slope = gelu_coef * (1.0 + 3.0 * 0.044715 * square)
    curve = 0.5 * (1.0 + level)
    d_curve = curve + 0.5 * gate * (1.0 - level * level) * slope
    d_gate_ref[...] = (d_mixed * up_ref[...] * d_curve).astype(bf16)
    d_up_ref[...] = (d_mixed * (gate * curve)).astype(bf16)


def mix_backward(d_out, down_mat, gate, upward):
    shapes = [jax.ShapeDtypeStruct(gate.shape, bf16)] * 2
    return pl.pallas_call(
        mix_back_kernel,
        grid=(gate.shape[1] // feed_tile,),
        in_specs=[
            whole_block(d_out),
            column_tile(down_mat),
            column_tile(gate),
            column_tile(upward),
        ],
        out_specs=[column_tile(shape) for shape in shapes],
        out_shape=shapes,
        name="mix_backward",
        **feed_params(),
    )(d_out, down_mat, gate, upward)


def spread_kernel(count, half, *refs):
    lefts, rights, outs = refs[:count], refs[count : 2 * count], refs[2 * count :]
    total = dotted(lefts[0][...], rights[0][...], 1, 1)
    for left, right in zip(lefts[1:], rights[1:]):
        total = total + dotted(left[...], right[...], 1, 1)
    for k, out in enumerate(outs):
        out[...] = total[k * half : (k + 1) * half].astype(out.dtype)


def product_blocks(lefts, rights, half):
    rows, width = lefts[0].shape[0], rights[0].shape[0]
    shapes = [
        jax.ShapeDtypeStruct((half, width), bf16 if k else f32) for k in range(rows // half)
    ]
    return pl.pallas_call(
        functools.partial(spread_kernel, len(lefts), half),
        grid=(width // feed_tile,),
        in_specs=[whole_block(left) for left in lefts] + [row_tile(right) for right in rights],
        out_specs=[column_tile(shape) for shape in shapes],
        out_shape=shapes,
        name="product_blocks",
        **feed_params(),
    )(*lefts, *rights)


def contract(left, right, left_dim, right_dim):
    return lax.dot_general(
        left, right, (((left_dim,), (right_dim,)), ((), ())), preferred_element_type=f32
    )


def body(
    layer_input,
    block_order,
    pre_attend,
    query_weight,
    key_weight,
    value_weight,
    output_weight,
    post_attend,
    pre_feed,
    gate_weight,
    up_weight,
    down_weight,
    post_feed,
    cotangent,
):
    _, rows, width = layer_input.shape
    block_len = LEN // block_order.shape[1]
    per_group = HQ // KV
    tensor_count = lax.axis_size("tensor")
    groups = KV // tensor_count
    factor = HD ** (-0.5)
    dp_count = lax.axis_size(("y", "core"))
    ctx_count = lax.axis_size("ctx")
    tensor_index = lax.axis_index("tensor")
    ctx_index = lax.axis_index("ctx")
    dp_index = lax.axis_index(("y", "core"))
    y_count = dp_count // cores
    y_index = dp_index // cores
    core_index = dp_index % cores
    dp_axes = ("y", "core")
    share = width // (dp_count * ctx_count)
    quarter = share * ctx_count
    half = rows // tensor_count
    pair = 2
    far_count = ctx_count // pair
    far_index = ctx_index // pair
    near_index = ctx_index % pair
    x_swap = [(0, 1), (1, 0)]
    all_swaps = {}
    for bz, bx in ((0, 1), (1, 0), (1, 1)):
        all_swaps[bz, bx] = [
            (c * 2 + t, (c ^ bz) * 2 + (t ^ bx)) for c in range(ctx_count) for t in range(2)
        ]
    near_swap = [(c, c ^ 1) for c in range(ctx_count)]

    def far_shift(step):
        return [
            (c, ((c // pair + step) % far_count) * pair + c % pair) for c in range(ctx_count)
        ]

    def along(dy, dc):
        pairs = []
        for y in range(y_count):
            for core in range(cores):
                target = ((y + dy) % y_count) * cores + (core + dc) % cores
                pairs.append((y * cores + core, target))
        return pairs

    def after(value, *others):
        return lax.optimization_barrier((value, *others))[0]

    def chosen(parts, index, place):
        count = len(parts)
        result = parts[0]
        for step in range(1, count):
            result = jnp.where((index - place) % count == step, parts[step], result)
        return result

    def in_order(parts, index):
        return jnp.concatenate([chosen(parts, index, k) for k in range(len(parts))], axis=0)

    def relative(values):
        first, second = values[:half], values[half:]
        flip = tensor_index == 1
        return jnp.concatenate(
            [jnp.where(flip, second, first), jnp.where(flip, first, second)], axis=0
        )

    def join(own):
        return jnp.concatenate([own, lax.ppermute(own, "tensor", x_swap)], axis=0)

    def join_absolute(own):
        return relative(join(own))

    def join_all(own):
        parts = [own]
        for pairs in all_swaps.values():
            parts.append(lax.ppermute(own, ("ctx", "tensor"), pairs))
        return jnp.concatenate(parts, axis=0)

    def pack_all(product):
        return [product[(k + 1) * half : (k + 2) * half].astype(bf16) for k in range(3)]

    def send_all(parts):
        return [
            lax.ppermute(part, ("ctx", "tensor"), pairs)
            for part, pairs in zip(parts, all_swaps.values())
        ]

    def sum_of(own, parts):
        for item in parts:
            own = own + item.astype(f32)
        return own

    all_pos = (
        block_order[0][:, None] * block_len + jnp.arange(block_len, dtype=jnp.int32)[None, :]
    ).reshape(ctx_count, tensor_count, half)
    all_pos = jnp.where(tensor_index == 1, all_pos[:, ::-1], all_pos).reshape(ctx_count, rows)
    local_pos = lax.dynamic_slice_in_dim(all_pos, ctx_index, 1, 0)[0]
    cosine, sine = rotary_tables(local_pos, HD)
    query_places = local_pos[None, :]
    key_places = all_pos.reshape(LEN, 1)

    both = ("y", "core", "ctx")
    gain_pack = jnp.stack([pre_attend, post_attend, pre_feed, post_feed], axis=1)
    gain_pack = jnp.pad(gain_pack, ((0, 0), (0, pad_lanes - 4)))
    heads_in_turn = []
    for g in range(groups):
        heads_in_turn += [
            key_weight[:, g * HD : (g + 1) * HD],
            value_weight[:, g * HD : (g + 1) * HD],
        ]
    keyvalue_pack = jnp.concatenate([*heads_in_turn, gain_pack], axis=1)
    keyvalue_all = lax.all_gather(keyvalue_pack, both, axis=0, tiled=True)
    query_mat = lax.all_gather(query_weight, both, axis=0, tiled=True)
    out_mat = lax.all_gather(output_weight.T, both, axis=0, tiled=True)

    hidden = gate_weight.shape[1] // pair
    is_high = near_index == 1

    def split(weight):
        low, high = weight[:, :hidden], weight[:, hidden:]
        return jnp.where(is_high, high, low), jnp.where(is_high, low, high)

    def far_pack(mine, got):
        return jnp.concatenate(
            [jnp.where(is_high, got, mine), jnp.where(is_high, mine, got)], axis=0
        )

    def far_start(block):
        return [lax.ppermute(block, "ctx", far_shift(s)) for s in range(1, far_count)]

    gate_mine, gate_other = split(gate_weight)
    up_mine, up_other = split(up_weight)
    down_mine, down_other = split(down_weight.T)
    gate_got = lax.ppermute(gate_other, "ctx", near_swap)
    rest_got = lax.ppermute(jnp.concatenate([up_other, down_other], axis=0), "ctx", near_swap)
    gate_block = far_pack(gate_mine, gate_got)
    gate_far = far_start(gate_block)
    up_block = far_pack(up_mine, rest_got[: rest_got.shape[0] // 2])
    down_block = far_pack(down_mine, rest_got[rest_got.shape[0] // 2 :])

    query_width = query_weight.shape[1]
    keyvalue_width = 2 * key_weight.shape[1]
    keyvalue_all = after(keyvalue_all, up_block, down_block)
    keyvalue_mat = keyvalue_all[:, :keyvalue_width]
    gains = keyvalue_all[:, keyvalue_width : keyvalue_width + 8].T.astype(f32)
    gain_in, gain_out, feed_gain, feed_post = gains[0], gains[1], gains[2], gains[3]

    inputs = relative(layer_input[0].astype(f32))
    own_inputs = inputs[:half]
    cot = lax.dynamic_slice_in_dim(cotangent[0], tensor_index * half, half, 0).astype(f32)

    attend_in = rms_norm(inputs, gain_in).astype(bf16)
    keyvalue_pre = jnp.dot(attend_in, keyvalue_mat, preferred_element_type=f32)
    turned = []
    for g in range(groups):
        middle = (2 * g + 1) * HD
        turned += [
            turn(keyvalue_pre[:, middle - HD : middle], cosine, sine),
            keyvalue_pre[:, middle : middle + HD],
        ]
    kv_local = jnp.concatenate(turned, axis=1).astype(bf16)

    from_left, from_right = [kv_local], [kv_local]

    def line_step(step, left_block, right_block):
        right_pairs = [(i, i + 1) for i in range(step - 1, ctx_count - 1)]
        left_pairs = [(i, i - 1) for i in range(1, ctx_count - step + 1)]
        from_left.append(lax.ppermute(left_block, "ctx", right_pairs))
        from_right.append(lax.ppermute(right_block, "ctx", left_pairs))

    line_step(1, kv_local, kv_local)
    gate_far = [after(part, kv_local) for part in gate_far]
    gate_rows = in_order([gate_block] + gate_far, far_index)
    gate_mat = lax.all_gather(gate_rows, dp_axes, axis=0, tiled=True)
    up_far = far_start(after(up_block, gate_rows))
    for step in range(2, ctx_count):
        left_block, right_block = from_left[-1], from_right[-1]
        if step == 2:
            left_block, right_block = after(left_block, gate_rows), after(right_block, gate_rows)
        line_step(step, left_block, right_block)
    last_blocks = (from_left[-2], from_right[-2])
    query_pre = jnp.dot(
        after(attend_in, *last_blocks), query_mat, preferred_element_type=f32
    )
    kv_parts = [kv_local]
    for step in range(1, ctx_count):
        kv_parts.append(
            jnp.where(ctx_index >= step, from_left[step], from_right[ctx_count - step])
        )
    kv_all = in_order(kv_parts, ctx_index)
    up_far = [after(part, *last_blocks) for part in up_far]
    up_rows = in_order([up_block] + up_far, far_index)
    up_mat = lax.all_gather(up_rows, dp_axes, axis=0, tiled=True)
    down_far = far_start(after(down_block, up_rows))
    kv_all = after(kv_all, up_rows)
    queries, attended_wide, attended, inverse_sums = attend_forward(
        query_pre, kv_all, cosine, sine, query_places, key_places, groups, per_group, ctx_count
    )
    other = contract(attended[half:], out_mat, 1, 1).astype(bf16)
    got = lax.ppermute(other, "tensor", x_swap)
    down_far = [after(part, got) for part in down_far]
    down_rows = in_order([down_block] + down_far, far_index)
    down_mat = lax.all_gather(down_rows, dp_axes, axis=0, tiled=True)
    attend_out = contract(attended[:half], out_mat, 1, 1) + got.astype(f32)
    hidden_mid = own_inputs + rms_norm(attend_out, gain_out)
    feed_own = rms_norm(hidden_mid, feed_gain).astype(bf16)
    feed_in = join_all(feed_own)
    gate, upward, mixed = mix_forward(feed_in, gate_mat, up_mat)
    feed_own, *sent = product_blocks([mixed], [down_mat], half)
    sent = send_all(sent)
    feed_left = feed_in
    feed_out = sum_of(feed_own, sent)
    layer_output = join_absolute(
        (hidden_mid + rms_norm(feed_out, feed_post)).astype(bf16)
    )[None]

    class Reduction:
        def __init__(self, left, right):
            self.whole = contract(left, right, 0, 0).astype(bf16)

        def piece(self, dy, dc):
            index = ((y_index + dy) % y_count) * cores + (core_index + dc) % cores
            return lax.dynamic_slice_in_dim(self.whole, index * quarter, quarter, 0)

        def core_pack(self):
            self.packed = [self.piece(dy, 1) for dy in range(y_count)]
            return self.packed

        def core_send(self):
            self.swapped = [lax.ppermute(p, dp_axes, along(0, 1)) for p in self.packed]

        def y_pack(self, *before):
            swapped = self.swapped
            if before:
                swapped = [after(item, *before) for item in swapped]
            self.packed = [
                (self.piece(dy, 0).astype(f32) + swapped[dy].astype(f32)).astype(bf16)
                for dy in range(1, y_count)
            ]
            return self.packed

        def y_send(self):
            self.arrived = [
                lax.ppermute(p, dp_axes, along(dy + 1, 0)) for dy, p in enumerate(self.packed)
            ]

        def sum_y(self, *before):
            arrived = self.arrived
            if before:
                arrived = [after(item, *before) for item in arrived]
            total = self.piece(0, 0).astype(f32) + self.swapped[0].astype(f32)
            self.total = sum_of(total, arrived).astype(bf16)
            return self.total

        def finish_ctx(self):
            return lax.psum_scatter(
                self.total, "ctx", scatter_dimension=0, tiled=True
            ).astype(f32)

        def block_of(self, index):
            result = self.blocks[0]
            for k in range(1, far_count):
                result = jnp.where(index == k, self.blocks[k], result)
            return result

        def far_pack(self, *before):
            total = self.sum_y(*before)
            self.blocks = [
                total[k * pair * share : (k + 1) * pair * share] for k in range(far_count)
            ]
            self.packed = [
                self.block_of((far_index + step) % far_count) for step in range(1, far_count)
            ]
            return self.packed

        def far_send(self):
            self.arrived = [
                lax.ppermute(p, "ctx", far_shift(s + 1)) for s, p in enumerate(self.packed)
            ]

        def near_pack(self, *before):
            arrived = self.arrived
            if before:
                arrived = [after(item, *before) for item in arrived]
            total = sum_of(self.block_of(far_index).astype(f32), arrived)
            low, high = total[:share], total[share:]
            self.own = jnp.where(is_high, high, low)
            self.other = jnp.where(is_high, low, high).astype(bf16)
            return self.other

    CoreReduction = Reduction

    def near_send(*sums):
        sent = sums[0].other
        if len(sums) > 1:
            sent = jnp.concatenate([item.other for item in sums], axis=0)
        got = lax.ppermute(sent, "ctx", near_swap).astype(f32)
        for k, item in enumerate(sums):
            item.got = got[k * share : (k + 1) * share]

    def finish_near(own, got):
        return jnp.concatenate(
            [jnp.where(is_high, got, own), jnp.where(is_high, own, got)], axis=1
        )

    def norm_back(values, gain, incoming):
        _, back = jax.vjp(rms_norm, values, gain)
        return back(incoming)

    d_feed_out, post_feed_part = norm_back(feed_out, feed_post, cot)
    d_feed_low = join_all(d_feed_out.astype(bf16))
    down_sum = Reduction(d_feed_low, mixed)
    down_sum.core_pack()
    down_sum.core_send()
    down_sum.y_pack()
    down_sum.y_send()
    d_feed_tied = after(d_feed_low, *down_sum.packed)
    d_gate, d_upward = mix_backward(d_feed_tied, down_mat, gate, upward)
    d_tied = (after(d_gate, *down_sum.packed), after(d_upward, *down_sum.packed))
    d_feed_own, *packed = product_blocks(d_tied, [gate_mat, up_mat], half)
    sent = send_all(packed)
    gate_sum = CoreReduction(after(feed_left, *packed), d_gate)
    gate_sum.core_pack()
    gate_sum.core_send()
    down_sum.far_pack(*gate_sum.packed)
    down_sum.far_send()
    up_sum = CoreReduction(after(feed_left, *down_sum.packed), d_upward)
    up_sum.core_pack()
    up_sum.core_send()
    gate_sum.y_pack(*up_sum.packed)
    gate_sum.y_send()
    own_feed = after(d_feed_own, *up_sum.packed, *gate_sum.packed)
    d_feed_in = sum_of(own_feed, sent)

    d_from_feed, pre_feed_part = norm_back(hidden_mid, feed_gain, d_feed_in)
    d_mid = cot + d_from_feed
    d_attend_out, post_attend_part = norm_back(attend_out, gain_out, d_mid)
    d_attend_own = d_attend_out.astype(bf16)
    d_attend_got = lax.ppermute(d_attend_own, "tensor", x_swap)
    up_sum.y_pack(d_attend_own)
    up_sum.y_send()
    d_attend_got = after(d_attend_got, *up_sum.packed)
    d_attend_low = jnp.concatenate([d_attend_own, d_attend_got], axis=0)
    d_attended = jnp.dot(d_attend_low, out_mat, preferred_element_type=f32).astype(bf16)
    out_sum = Reduction(after(d_attend_low, d_attended), attended)
    out_sum.core_pack()
    out_sum.core_send()
    gate_sum.far_pack(*out_sum.packed)
    gate_sum.far_send()
    d_attended = after(d_attended, *gate_sum.packed)
    d_attended = after(d_attended, *down_sum.arrived)
    d_query_pre, d_kv = attend_backward(
        queries,
        kv_all,
        d_attended,
        attended_wide,
        inverse_sums,
        cosine,
        sine,
        query_places,
        key_places,
        groups,
        per_group,
        ctx_count,
    )
    d_kv = after(d_kv, *gate_sum.arrived)
    d_kv_local = lax.psum_scatter(d_kv, "ctx", scatter_dimension=0, tiled=True).astype(f32)
    out_sum.y_pack(d_kv)
    out_sum.y_send()
    query_sum = Reduction(after(attend_in, *out_sum.packed), d_query_pre)
    query_sum.core_pack()
    query_sum.core_send()
    last = query_sum.packed
    down_sum.near_pack(*query_sum.packed)
    near_send(down_sum)
    last = [down_sum.other]
    query_sum.y_pack(*last)
    query_sum.y_send()
    query_part = contract(after(d_query_pre, *query_sum.packed), query_mat, 1, 1)
    last = [query_part]
    up_sum.far_pack(query_part)
    up_sum.far_send()
    last = up_sum.packed
    gate_sum.near_pack(*last)
    near_send(gate_sum)
    last = [gate_sum.other]
    out_sum.sum_y(*last)
    d_kv_local = after(d_kv_local, out_sum.total)
    turned = []
    for g in range(groups):
        middle = (2 * g + 1) * HD
        turned += [
            turn(d_kv_local[:, middle - HD : middle], cosine, -sine),
            d_kv_local[:, middle : middle + HD],
        ]
    d_keyvalue = jnp.concatenate(turned, axis=1).astype(bf16)

    keyvalue_sum = Reduction(attend_in, d_keyvalue)
    keyvalue_sum.core_pack()
    keyvalue_sum.core_send()
    keyvalue_part = contract(
        after(d_keyvalue, *keyvalue_sum.packed), keyvalue_mat, 1, 1
    )
    d_attend_part = query_part + keyvalue_part
    d_attend_sent = d_attend_part[half:].astype(bf16)
    got = lax.ppermute(d_attend_sent, "tensor", x_swap)
    keyvalue_sum.y_pack(d_attend_sent)
    keyvalue_sum.y_send()
    query_sum.sum_y(d_keyvalue)
    up_sum.near_pack(*keyvalue_sum.packed)
    near_send(up_sum)
    keyvalue_sum.sum_y()
    joint = jnp.concatenate([out_sum.total, query_sum.total], axis=1)
    joint = lax.psum_scatter(joint, "ctx", scatter_dimension=0, tiled=True).astype(f32)
    joint = after(joint, keyvalue_sum.total)
    out_grad, query_grad = joint[:, :query_width].T, joint[:, query_width:]
    attend_grad = keyvalue_sum.finish_ctx()

    in_factor = lax.rsqrt(jnp.mean(inputs * inputs, axis=-1, keepdims=True) + epsilon)
    pre_attend_part = jnp.sum(
        after(d_attend_part, keyvalue_sum.total) * inputs * in_factor, axis=0
    )
    gain_grads = jnp.stack([pre_attend_part, post_attend_part, pre_feed_part, post_feed_part])

    def swap_sum(values, axis, count):
        bit = 1
        while bit < count:
            pairs = [(i, i ^ bit) for i in range(count)]
            values = values + lax.ppermute(values, axis, pairs)
            bit *= 2
        return values

    gain_grads = swap_sum(gain_grads, dp_axes, dp_count)
    gain_grads = swap_sum(gain_grads, "ctx", ctx_count)
    gain_grads = swap_sum(gain_grads, "tensor", tensor_count)
    place = dp_index * ctx_count + ctx_index
    gain_grads = gain_grads.reshape(4, dp_count * ctx_count, share)
    gain_grads = lax.dynamic_slice_in_dim(gain_grads, place, 1, 1)[:, 0]

    down_grad = finish_near(down_sum.own, down_sum.got).T
    gate_grad = finish_near(gate_sum.own, gate_sum.got)
    up_grad = finish_near(up_sum.own, up_sum.got)
    key_grad = jnp.concatenate(
        [attend_grad[:, 2 * g * HD : (2 * g + 1) * HD] for g in range(groups)], axis=1
    )
    value_grad = jnp.concatenate(
        [attend_grad[:, (2 * g + 1) * HD : (2 * g + 2) * HD] for g in range(groups)], axis=1
    )

    d_attend_in = after(d_attend_part[:half], *keyvalue_sum.packed) + got.astype(f32)
    d_from_attend, _ = norm_back(own_inputs, gain_in, d_attend_in)
    input_grad = join_absolute((d_mid + d_from_attend).astype(bf16)).astype(f32)[None]

    return (
        layer_output,
        input_grad,
        gain_grads[0],
        query_grad,
        key_grad,
        value_grad,
        out_grad,
        gain_grads[1],
        gain_grads[2],
        gate_grad,
        up_grad,
        down_grad,
        gain_grads[3],
    )


def solution(mesh):
    dp_count, ctx_count, tensor_count = mesh.devices.shape
    mesh = jax.sharding.Mesh(
        mesh.devices.reshape(dp_count // cores, cores, ctx_count, tensor_count),
        ("y", "core", "ctx", "tensor"),
    )
    dp = ("y", "core")
    both = ("y", "core", "ctx")
    return jax.shard_map(
        body,
        mesh=mesh,
        in_specs=(
            P(dp, "ctx", None),
            P(dp, None),
            P(both),
            P(both, "tensor"),
            P(both, "tensor"),
            P(both, "tensor"),
            P("tensor", both),
            P(both),
            P(both),
            P(both, "tensor"),
            P(both, "tensor"),
            P("tensor", both),
            P(both),
            P(dp, "ctx", None),
        ),
        out_specs=(
            P(dp, "ctx", None),
            P(dp, "ctx", None),
            P(both),
            P(both, "tensor"),
            P(both, "tensor"),
            P(both, "tensor"),
            P("tensor", both),
            P(both),
            P(both),
            P(both, "tensor"),
            P(both, "tensor"),
            P("tensor", both),
            P(both),
        ),
        check_vma=False,
    )
```

```python
import functools

import jax
import jax.numpy as jnp
from jax import lax
from jax.experimental import pallas as pl
from jax.experimental.pallas import tpu as pltpu
from jax.sharding import PartitionSpec as P

HQ = 8
KV = 4
HD = 256
LEN = 2048

epsilon = 1e-06
cap_value = 50.0
gelu_coef = 0.7978845608028654
cores = 2
pad_lanes = 128

f32 = jnp.float32
bf16 = jnp.bfloat16


def rms_norm(values, gain):
    factor = lax.rsqrt(jnp.mean(values * values, axis=-1, keepdims=True) + epsilon)
    return values * factor * gain


def gelu_tanh(values):
    return (
        0.5 * values * (1.0 + jnp.tanh(gelu_coef * (values + 0.044715 * values * values * values)))
    )


def gated_product(gate, upward):
    return gelu_tanh(gate) * upward


def rotary_tables(positions, head_size):
    half = head_size // 2
    freqs = 10000.0 ** (-(jnp.arange(half, dtype=f32) * 2.0) / head_size)
    angle = positions.astype(f32)[:, None] * freqs[None, :]
    return (jnp.cos(angle), jnp.sin(angle))


attend_limit = 48 * 1024 * 1024


def dotted(left, right, left_dim, right_dim, precision=None):
    return lax.dot_general(
        left,
        right,
        (((left_dim,), (right_dim,)), ((), ())),
        precision=precision,
        preferred_element_type=f32,
    )


def turn(values, cosine, sine):
    half = HD // 2
    first, second = values[:, :half], values[:, half:]
    return jnp.concatenate(
        [first * cosine - second * sine, second * cosine + first * sine], axis=1
    )


def forward_kernel(chunks, pre_ref, kv_ref, cos_ref, sin_ref, qpos_ref, kpos_ref, q_ref, out_ref, low_ref, inv_ref):
    rows = pre_ref.shape[0]
    size = kv_ref.shape[0] // chunks
    q = turn(pre_ref[...], cos_ref[...], sin_ref[...]).astype(bf16)
    q_ref[...] = q
    qpos = qpos_ref[...]
    total = jnp.zeros((1, rows), f32)
    acc = jnp.zeros((HD, rows), f32)
    for c in range(chunks):
        part = pl.ds(c * size, size)
        raw = dotted(kv_ref[part, :HD], q, 1, 1)
        level = jnp.tanh(raw * (HD ** (-0.5) / cap_value))
        weight = jnp.where(qpos >= kpos_ref[part, :], jnp.exp(cap_value * level), 0.0)
        total = total + jnp.sum(weight, axis=0, keepdims=True)
        acc = acc + dotted(kv_ref[part, HD:], weight.astype(bf16), 0, 0)
    inverse = 1.0 / total
    inv_ref[0] = inverse
    out = (acc * inverse).T
    out_ref[...] = out
    low_ref[...] = out.astype(bf16)


def attend_forward(query_pre, kv_all, cosine, sine, qpos, kpos, groups, per_group, chunks):
    rows, width = query_pre.shape
    length = kv_all.shape[0]
    heads = groups * per_group
    by_head = pl.BlockSpec((rows, HD), lambda g, r: (0, g * per_group + r))
    fixed = lambda shape: pl.BlockSpec(shape, lambda g, r: (0, 0))
    return pl.pallas_call(
        functools.partial(forward_kernel, chunks),
        grid=(groups, per_group),
        in_specs=[
            by_head,
            pl.BlockSpec((length, 2 * HD), lambda g, r: (0, g)),
            fixed((rows, HD // 2)),
            fixed((rows, HD // 2)),
            fixed((1, rows)),
            fixed((length, 1)),
        ],
        out_specs=[
            by_head,
            by_head,
            by_head,
            pl.BlockSpec((1, 1, rows), lambda g, r: (g * per_group + r, 0, 0)),
        ],
        out_shape=[
            jax.ShapeDtypeStruct((rows, width), bf16),
            jax.ShapeDtypeStruct((rows, width), f32),
            jax.ShapeDtypeStruct((rows, width), bf16),
            jax.ShapeDtypeStruct((heads, 1, rows), f32),
        ],
        compiler_params=pltpu.CompilerParams(vmem_limit_bytes=attend_limit),
        cost_estimate=pl.CostEstimate(
            flops=rows * width,
            bytes_accessed=rows * width,
            transcendentals=0,
        ),
        name="attend_forward",
    )(query_pre, kv_all, cosine, sine, qpos, kpos)


def backward_kernel(per_group, q_ref, kv_ref, da_ref, out_ref, inv_ref, cos_ref, sin_ref, qpos_ref, kpos_ref, dq_ref, dkv_ref, delta_ref, sum_ref, both_ref):
    c, r = pl.program_id(1), pl.program_id(2)
    q, da = q_ref[...], da_ref[...]
    k, v = kv_ref[:, :HD], kv_ref[:, HD:]

    @pl.when(c == 0)
    def _():
        delta_ref[r] = dotted(
            jnp.ones((8, HD), f32), da.astype(f32) * out_ref[...], 1, 1, lax.Precision.HIGHEST
        )

    delta = delta_ref[r][0:1]
    level = jnp.tanh(dotted(k, q, 1, 1) * (HD ** (-0.5) / cap_value))
    seen = qpos_ref[...] >= kpos_ref[...]
    prob = jnp.where(seen, jnp.exp(cap_value * level), 0.0) * inv_ref[0]
    d_prob = dotted(v, da, 1, 1)
    d_raw = (prob * (d_prob - delta) * (1.0 - level * level)).astype(bf16)
    d_key = dotted(d_raw, q, 1, 0) * HD ** (-0.5)
    d_value = dotted(prob.astype(bf16), da, 1, 0)
    d_query = dotted(d_raw, k, 0, 0)

    @pl.when(r == 0)
    def _():
        both_ref[:, :HD] = d_key
        both_ref[:, HD:] = d_value

    @pl.when(r > 0)
    def _():
        both_ref[:, :HD] += d_key
        both_ref[:, HD:] += d_value

    @pl.when(r == per_group - 1)
    def _():
        dkv_ref[...] = both_ref[...].astype(bf16)

    @pl.when(c == 0)
    def _():
        sum_ref[r] = d_query

    @pl.when(c > 0)
    def _():
        sum_ref[r] += d_query

    for head in range(per_group):

        @pl.when((c == pl.num_programs(1) - 1) & (r == head))
        def _():
            whole = sum_ref[head] * HD ** (-0.5)
            dq_ref[:, head * HD : (head + 1) * HD] = turn(
                whole, cos_ref[...], -sin_ref[...]
            ).astype(bf16)


def attend_backward(queries, kv_all, d_attended, out, inverse, cosine, sine, qpos, kpos, groups, per_group, chunks):
    rows, width = queries.shape
    length = kv_all.shape[0]
    size = length // chunks
    heads = groups * per_group
    by_head = pl.BlockSpec((rows, HD), lambda g, c, r: (0, g * per_group + r))
    fixed = lambda shape: pl.BlockSpec(shape, lambda g, c, r: (0, 0))
    by_chunk = pl.BlockSpec((size, 2 * HD), lambda g, c, r: (c, g))
    return pl.pallas_call(
        functools.partial(backward_kernel, per_group),
        grid=(groups, chunks, per_group),
        in_specs=[
            by_head,
            by_chunk,
            by_head,
            by_head,
            pl.BlockSpec((1, 1, rows), lambda g, c, r: (g * per_group + r, 0, 0)),
            fixed((rows, HD // 2)),
            fixed((rows, HD // 2)),
            fixed((1, rows)),
            pl.BlockSpec((size, 1), lambda g, c, r: (c, 0)),
        ],
        out_specs=[
            pl.BlockSpec((rows, per_group * HD), lambda g, c, r: (0, g)),
            by_chunk,
        ],
        out_shape=[
            jax.ShapeDtypeStruct((rows, width), bf16),
            jax.ShapeDtypeStruct((length, groups * 2 * HD), bf16),
        ],
        scratch_shapes=[
            pltpu.VMEM((per_group, 8, rows), f32),
            pltpu.VMEM((per_group, rows, HD), f32),
            pltpu.VMEM((size, 2 * HD), f32),
        ],
        compiler_params=pltpu.CompilerParams(vmem_limit_bytes=attend_limit),
        cost_estimate=pl.CostEstimate(
            flops=rows * width,
            bytes_accessed=rows * width,
            transcendentals=0,
        ),
        name="attend_backward",
    )(queries, kv_all, d_attended, out, inverse, cosine, sine, qpos, kpos)


feed_limit = 56 * 1024 * 1024
feed_tile = 256


def feed_params():
    return dict(
        compiler_params=pltpu.CompilerParams(vmem_limit_bytes=feed_limit),
        cost_estimate=pl.CostEstimate(flops=1000000, bytes_accessed=1000000, transcendentals=0),
    )


def whole_block(array):
    return pl.BlockSpec(array.shape, lambda n: (0, 0))


def column_tile(array):
    return pl.BlockSpec((array.shape[0], feed_tile), lambda n: (0, n))


def row_tile(array):
    return pl.BlockSpec((feed_tile, array.shape[1]), lambda n: (n, 0))


def mix_kernel(x_ref, gate_mat_ref, up_mat_ref, gate_ref, up_ref, mixed_ref):
    x = x_ref[...]
    gate = dotted(x, gate_mat_ref[...], 1, 0)
    upward = dotted(x, up_mat_ref[...], 1, 0)
    gate_ref[...] = gate
    up_ref[...] = upward
    inner = gelu_coef * (gate + 0.044715 * gate * gate * gate)
    mixed_ref[...] = (0.5 * gate * (1.0 + jnp.tanh(inner)) * upward).astype(bf16)


def mix_forward(x, gate_mat, up_mat):
    rows, hidden = x.shape[0], gate_mat.shape[1]
    shapes = [jax.ShapeDtypeStruct((rows, hidden), kind) for kind in (f32, f32, bf16)]
    return pl.pallas_call(
        mix_kernel,
        grid=(hidden // feed_tile,),
        in_specs=[whole_block(x), column_tile(gate_mat), column_tile(up_mat)],
        out_specs=[column_tile(shape) for shape in shapes],
        out_shape=shapes,
        name="mix_forward",
        **feed_params(),
    )(x, gate_mat, up_mat)


def mix_back_kernel(d_ref, down_mat_ref, gate_ref, up_ref, d_gate_ref, d_up_ref):
    d_mixed = dotted(d_ref[...], down_mat_ref[...], 1, 0)
    gate = gate_ref[...]
    square = gate * gate
    level = jnp.tanh(gelu_coef * gate * (1.0 + 0.044715 * square))
    slope = gelu_coef * (1.0 + 3.0 * 0.044715 * square)
    curve = 0.5 * (1.0 + level)
    d_curve = curve + 0.5 * gate * (1.0 - level * level) * slope
    d_gate_ref[...] = (d_mixed * up_ref[...] * d_curve).astype(bf16)
    d_up_ref[...] = (d_mixed * (gate * curve)).astype(bf16)


def mix_backward(d_out, down_mat, gate, upward):
    shapes = [jax.ShapeDtypeStruct(gate.shape, bf16)] * 2
    return pl.pallas_call(
        mix_back_kernel,
        grid=(gate.shape[1] // feed_tile,),
        in_specs=[
            whole_block(d_out),
            column_tile(down_mat),
            column_tile(gate),
            column_tile(upward),
        ],
        out_specs=[column_tile(shape) for shape in shapes],
        out_shape=shapes,
        name="mix_backward",
        **feed_params(),
    )(d_out, down_mat, gate, upward)


def spread_kernel(count, half, *refs):
    lefts, rights, outs = refs[:count], refs[count : 2 * count], refs[2 * count :]
    total = dotted(lefts[0][...], rights[0][...], 1, 1)
    for left, right in zip(lefts[1:], rights[1:]):
        total = total + dotted(left[...], right[...], 1, 1)
    for k, out in enumerate(outs):
        out[...] = total[k * half : (k + 1) * half].astype(out.dtype)


def product_blocks(lefts, rights, half):
    rows, width = lefts[0].shape[0], rights[0].shape[0]
    shapes = [
        jax.ShapeDtypeStruct((half, width), bf16 if k else f32) for k in range(rows // half)
    ]
    return pl.pallas_call(
        functools.partial(spread_kernel, len(lefts), half),
        grid=(width // feed_tile,),
        in_specs=[whole_block(left) for left in lefts] + [row_tile(right) for right in rights],
        out_specs=[column_tile(shape) for shape in shapes],
        out_shape=shapes,
        name="product_blocks",
        **feed_params(),
    )(*lefts, *rights)


def contract(left, right, left_dim, right_dim):
    return lax.dot_general(
        left, right, (((left_dim,), (right_dim,)), ((), ())), preferred_element_type=f32
    )


def body(
    layer_input,
    block_order,
    pre_attend,
    query_weight,
    key_weight,
    value_weight,
    output_weight,
    post_attend,
    pre_feed,
    gate_weight,
    up_weight,
    down_weight,
    post_feed,
    cotangent,
):
    _, rows, width = layer_input.shape
    block_len = LEN // block_order.shape[1]
    per_group = HQ // KV
    tensor_count = lax.axis_size("tensor")
    groups = KV // tensor_count
    factor = HD ** (-0.5)
    dp_count = lax.axis_size(("y", "core"))
    ctx_count = lax.axis_size("ctx")
    tensor_index = lax.axis_index("tensor")
    ctx_index = lax.axis_index("ctx")
    dp_index = lax.axis_index(("y", "core"))
    y_count = dp_count // cores
    y_index = dp_index // cores
    core_index = dp_index % cores
    dp_axes = ("y", "core")
    share = width // (dp_count * ctx_count)
    quarter = share * ctx_count
    half = rows // tensor_count
    pair = 2
    far_count = ctx_count // pair
    far_index = ctx_index // pair
    near_index = ctx_index % pair
    x_swap = [(0, 1), (1, 0)]
    all_swaps = {}
    for bz, bx in ((0, 1), (1, 0), (1, 1)):
        all_swaps[bz, bx] = [
            (c * 2 + t, (c ^ bz) * 2 + (t ^ bx)) for c in range(ctx_count) for t in range(2)
        ]
    near_swap = [(c, c ^ 1) for c in range(ctx_count)]

    def far_shift(step):
        return [
            (c, ((c // pair + step) % far_count) * pair + c % pair) for c in range(ctx_count)
        ]

    def along(dy, dc):
        pairs = []
        for y in range(y_count):
            for core in range(cores):
                target = ((y + dy) % y_count) * cores + (core + dc) % cores
                pairs.append((y * cores + core, target))
        return pairs

    def after(value, *others):
        return lax.optimization_barrier((value, *others))[0]

    def chosen(parts, index, place):
        count = len(parts)
        result = parts[0]
        for step in range(1, count):
            result = jnp.where((index - place) % count == step, parts[step], result)
        return result

    def in_order(parts, index):
        return jnp.concatenate([chosen(parts, index, k) for k in range(len(parts))], axis=0)

    def relative(values):
        first, second = values[:half], values[half:]
        flip = tensor_index == 1
        return jnp.concatenate(
            [jnp.where(flip, second, first), jnp.where(flip, first, second)], axis=0
        )

    def join(own):
        return jnp.concatenate([own, lax.ppermute(own, "tensor", x_swap)], axis=0)

    def join_absolute(own):
        return relative(join(own))

    def join_all(own):
        parts = [own]
        for pairs in all_swaps.values():
            parts.append(lax.ppermute(own, ("ctx", "tensor"), pairs))
        return jnp.concatenate(parts, axis=0)

    def pack_all(product):
        return [product[(k + 1) * half : (k + 2) * half].astype(bf16) for k in range(3)]

    def send_all(parts):
        return [
            lax.ppermute(part, ("ctx", "tensor"), pairs)
            for part, pairs in zip(parts, all_swaps.values())
        ]

    part = half // 2

    def hop(values, bz, bx):
        return lax.ppermute(values, ("ctx", "tensor"), all_swaps[bz, bx])

    def join_by_hops(own):
        beside, below = hop(own, 0, 1), hop(own, 1, 0)
        corner = [hop(beside[:part], 1, 0), hop(below[part:], 0, 1)]
        return jnp.concatenate([own, beside, below, *corner], axis=0)

    def send_by_hops(parts):
        beside, below, corner = parts
        by_side, by_below = hop(corner[:part], 0, 1), hop(corner[part:], 1, 0)

        def joined(values, got):
            return (values.astype(f32) + got.astype(f32)).astype(bf16)

        below = jnp.concatenate([joined(below[:part], by_side), below[part:]], axis=0)
        beside = jnp.concatenate([beside[:part], joined(beside[part:], by_below)], axis=0)
        return [hop(below, 1, 0), hop(beside, 0, 1)]

    def sum_of(own, parts):
        for item in parts:
            own = own + item.astype(f32)
        return own

    all_pos = (
        block_order[0][:, None] * block_len + jnp.arange(block_len, dtype=jnp.int32)[None, :]
    ).reshape(ctx_count, tensor_count, half)
    all_pos = jnp.where(tensor_index == 1, all_pos[:, ::-1], all_pos).reshape(ctx_count, rows)
    local_pos = lax.dynamic_slice_in_dim(all_pos, ctx_index, 1, 0)[0]
    cosine, sine = rotary_tables(local_pos, HD)
    query_places = local_pos[None, :]
    key_places = all_pos.reshape(LEN, 1)

    both = ("y", "core", "ctx")
    gain_pack = jnp.stack([pre_attend, post_attend, pre_feed, post_feed], axis=1)
    gain_pack = jnp.pad(gain_pack, ((0, 0), (0, pad_lanes - 4)))
    heads_in_turn = []
    for g in range(groups):
        heads_in_turn += [
            key_weight[:, g * HD : (g + 1) * HD],
            value_weight[:, g * HD : (g + 1) * HD],
        ]
    keyvalue_pack = jnp.concatenate([*heads_in_turn, gain_pack], axis=1)
    keyvalue_all = lax.all_gather(keyvalue_pack, both, axis=0, tiled=True)
    query_mat = lax.all_gather(query_weight, both, axis=0, tiled=True)
    out_mat = lax.all_gather(output_weight.T, both, axis=0, tiled=True)

    hidden = gate_weight.shape[1] // pair
    is_high = near_index == 1

    def split(weight):
        low, high = weight[:, :hidden], weight[:, hidden:]
        return jnp.where(is_high, high, low), jnp.where(is_high, low, high)

    def far_pack(mine, got):
        return jnp.concatenate(
            [jnp.where(is_high, got, mine), jnp.where(is_high, mine, got)], axis=0
        )

    def far_start(block):
        return [lax.ppermute(block, "ctx", far_shift(s)) for s in range(1, far_count)]

    gate_mine, gate_other = split(gate_weight)
    up_mine, up_other = split(up_weight)
    down_mine, down_other = split(down_weight.T)
    gate_got = lax.ppermute(gate_other, "ctx", near_swap)
    rest_got = lax.ppermute(jnp.concatenate([up_other, down_other], axis=0), "ctx", near_swap)
    gate_block = far_pack(gate_mine, gate_got)
    gate_far = far_start(gate_block)
    up_block = far_pack(up_mine, rest_got[: rest_got.shape[0] // 2])
    down_block = far_pack(down_mine, rest_got[rest_got.shape[0] // 2 :])

    query_width = query_weight.shape[1]
    keyvalue_width = 2 * key_weight.shape[1]
    keyvalue_all = after(keyvalue_all, up_block, down_block)
    keyvalue_mat = keyvalue_all[:, :keyvalue_width]
    gains = keyvalue_all[:, keyvalue_width : keyvalue_width + 8].T.astype(f32)
    gain_in, gain_out, feed_gain, feed_post = gains[0], gains[1], gains[2], gains[3]

    inputs = relative(layer_input[0].astype(f32))
    own_inputs = inputs[:half]
    cot = lax.dynamic_slice_in_dim(cotangent[0], tensor_index * half, half, 0).astype(f32)

    attend_in = rms_norm(inputs, gain_in).astype(bf16)
    keyvalue_pre = jnp.dot(attend_in, keyvalue_mat, preferred_element_type=f32)
    turned = []
    for g in range(groups):
        middle = (2 * g + 1) * HD
        turned += [
            turn(keyvalue_pre[:, middle - HD : middle], cosine, sine),
            keyvalue_pre[:, middle : middle + HD],
        ]
    kv_local = jnp.concatenate(turned, axis=1).astype(bf16)

    from_left, from_right = [kv_local], [kv_local]

    def line_step(step, left_block, right_block):
        right_pairs = [(i, i + 1) for i in range(step - 1, ctx_count - 1)]
        left_pairs = [(i, i - 1) for i in range(1, ctx_count - step + 1)]
        from_left.append(lax.ppermute(left_block, "ctx", right_pairs))
        from_right.append(lax.ppermute(right_block, "ctx", left_pairs))

    line_step(1, kv_local, kv_local)
    gate_far = [after(part, kv_local) for part in gate_far]
    gate_rows = in_order([gate_block] + gate_far, far_index)
    gate_mat = lax.all_gather(gate_rows, dp_axes, axis=0, tiled=True)
    up_far = far_start(after(up_block, gate_rows))
    for step in range(2, ctx_count):
        left_block, right_block = from_left[-1], from_right[-1]
        if step == 2:
            left_block, right_block = after(left_block, gate_rows), after(right_block, gate_rows)
        line_step(step, left_block, right_block)
    last_blocks = (from_left[-2], from_right[-2])
    query_pre = jnp.dot(
        after(attend_in, *last_blocks), query_mat, preferred_element_type=f32
    )
    kv_parts = [kv_local]
    for step in range(1, ctx_count):
        kv_parts.append(
            jnp.where(ctx_index >= step, from_left[step], from_right[ctx_count - step])
        )
    kv_all = in_order(kv_parts, ctx_index)
    up_far = [after(part, *last_blocks) for part in up_far]
    up_rows = in_order([up_block] + up_far, far_index)
    up_mat = lax.all_gather(up_rows, dp_axes, axis=0, tiled=True)
    down_far = far_start(after(down_block, up_rows))
    kv_all = after(kv_all, up_rows)
    queries, attended_wide, attended, inverse_sums = attend_forward(
        query_pre, kv_all, cosine, sine, query_places, key_places, groups, per_group, ctx_count
    )
    other = contract(attended[half:], out_mat, 1, 1).astype(bf16)
    got = lax.ppermute(other, "tensor", x_swap)
    down_far = [after(part, got) for part in down_far]
    down_rows = in_order([down_block] + down_far, far_index)
    down_mat = lax.all_gather(down_rows, dp_axes, axis=0, tiled=True)
    attend_out = contract(attended[:half], out_mat, 1, 1) + got.astype(f32)
    hidden_mid = own_inputs + rms_norm(attend_out, gain_out)
    feed_own = rms_norm(hidden_mid, feed_gain).astype(bf16)
    feed_in = join_by_hops(feed_own)
    gate, upward, mixed = mix_forward(feed_in, gate_mat, up_mat)
    feed_own, *sent = product_blocks([mixed], [down_mat], half)
    sent = send_by_hops(sent)
    feed_left = feed_in
    feed_out = sum_of(feed_own, sent)
    layer_output = join_absolute(
        (hidden_mid + rms_norm(feed_out, feed_post)).astype(bf16)
    )[None]

    class Reduction:
        def __init__(self, left, right):
            self.whole = contract(left, right, 0, 0).astype(bf16)

        def piece(self, dy, dc):
            index = ((y_index + dy) % y_count) * cores + (core_index + dc) % cores
            return lax.dynamic_slice_in_dim(self.whole, index * quarter, quarter, 0)

        def core_pack(self):
            self.packed = [self.piece(dy, 1) for dy in range(y_count)]
            return self.packed

        def core_send(self):
            self.swapped = [lax.ppermute(p, dp_axes, along(0, 1)) for p in self.packed]

        def y_pack(self, *before):
            swapped = self.swapped
            if before:
                swapped = [after(item, *before) for item in swapped]
            self.packed = [
                (self.piece(dy, 0).astype(f32) + swapped[dy].astype(f32)).astype(bf16)
                for dy in range(1, y_count)
            ]
            return self.packed

        def y_send(self):
            self.arrived = [
                lax.ppermute(p, dp_axes, along(dy + 1, 0)) for dy, p in enumerate(self.packed)
            ]

        def sum_y(self, *before):
            arrived = self.arrived
            if before:
                arrived = [after(item, *before) for item in arrived]
            total = self.piece(0, 0).astype(f32) + self.swapped[0].astype(f32)
            self.total = sum_of(total, arrived).astype(bf16)
            return self.total

        def finish_ctx(self):
            return lax.psum_scatter(
                self.total, "ctx", scatter_dimension=0, tiled=True
            ).astype(f32)

        def block_of(self, index):
            result = self.blocks[0]
            for k in range(1, far_count):
                result = jnp.where(index == k, self.blocks[k], result)
            return result

        def far_pack(self, *before):
            total = self.sum_y(*before)
            self.blocks = [
                total[k * pair * share : (k + 1) * pair * share] for k in range(far_count)
            ]
            self.packed = [
                self.block_of((far_index + step) % far_count) for step in range(1, far_count)
            ]
            return self.packed

        def far_send(self):
            self.arrived = [
                lax.ppermute(p, "ctx", far_shift(s + 1)) for s, p in enumerate(self.packed)
            ]

        def near_pack(self, *before):
            arrived = self.arrived
            if before:
                arrived = [after(item, *before) for item in arrived]
            total = sum_of(self.block_of(far_index).astype(f32), arrived)
            low, high = total[:share], total[share:]
            self.own = jnp.where(is_high, high, low)
            self.other = jnp.where(is_high, low, high).astype(bf16)
            return self.other

    CoreReduction = Reduction

    def near_send(*sums):
        sent = sums[0].other
        if len(sums) > 1:
            sent = jnp.concatenate([item.other for item in sums], axis=0)
        got = lax.ppermute(sent, "ctx", near_swap).astype(f32)
        for k, item in enumerate(sums):
            item.got = got[k * share : (k + 1) * share]

    def finish_near(own, got):
        return jnp.concatenate(
            [jnp.where(is_high, got, own), jnp.where(is_high, own, got)], axis=1
        )

    def norm_back(values, gain, incoming):
        _, back = jax.vjp(rms_norm, values, gain)
        return back(incoming)

    d_feed_out, post_feed_part = norm_back(feed_out, feed_post, cot)
    d_feed_low = join_by_hops(d_feed_out.astype(bf16))
    down_sum = Reduction(d_feed_low, mixed)
    down_sum.core_pack()
    down_sum.core_send()
    down_sum.y_pack()
    down_sum.y_send()
    d_feed_tied = after(d_feed_low, *down_sum.packed)
    d_gate, d_upward = mix_backward(d_feed_tied, down_mat, gate, upward)
    d_tied = (after(d_gate, *down_sum.packed), after(d_upward, *down_sum.packed))
    d_feed_own, *packed = product_blocks(d_tied, [gate_mat, up_mat], half)
    sent = send_all(packed)
    gate_sum = CoreReduction(after(feed_left, *packed), d_gate)
    gate_sum.core_pack()
    gate_sum.core_send()
    down_sum.far_pack(*gate_sum.packed)
    down_sum.far_send()
    up_sum = CoreReduction(after(feed_left, *down_sum.packed), d_upward)
    up_sum.core_pack()
    up_sum.core_send()
    gate_sum.y_pack(*up_sum.packed)
    gate_sum.y_send()
    own_feed = after(d_feed_own, *up_sum.packed, *gate_sum.packed)
    d_feed_in = sum_of(own_feed, sent)

    d_from_feed, pre_feed_part = norm_back(hidden_mid, feed_gain, d_feed_in)
    d_mid = cot + d_from_feed
    d_attend_out, post_attend_part = norm_back(attend_out, gain_out, d_mid)
    d_attend_own = d_attend_out.astype(bf16)
    d_attend_got = lax.ppermute(d_attend_own, "tensor", x_swap)
    up_sum.y_pack(d_attend_own)
    up_sum.y_send()
    d_attend_got = after(d_attend_got, *up_sum.packed)
    d_attend_low = jnp.concatenate([d_attend_own, d_attend_got], axis=0)
    d_attended = jnp.dot(d_attend_low, out_mat, preferred_element_type=f32).astype(bf16)
    out_sum = Reduction(after(d_attend_low, d_attended), attended)
    out_sum.core_pack()
    out_sum.core_send()
    gate_sum.far_pack(*out_sum.packed)
    gate_sum.far_send()
    d_attended = after(d_attended, *gate_sum.packed)
    d_attended = after(d_attended, *down_sum.arrived)
    d_query_pre, d_kv = attend_backward(
        queries,
        kv_all,
        d_attended,
        attended_wide,
        inverse_sums,
        cosine,
        sine,
        query_places,
        key_places,
        groups,
        per_group,
        ctx_count,
    )
    d_kv = after(d_kv, *gate_sum.arrived)
    d_kv_local = lax.psum_scatter(d_kv, "ctx", scatter_dimension=0, tiled=True).astype(f32)
    out_sum.y_pack(d_kv)
    out_sum.y_send()
    query_sum = Reduction(after(attend_in, *out_sum.packed), d_query_pre)
    query_sum.core_pack()
    query_sum.core_send()
    last = query_sum.packed
    down_sum.near_pack(*query_sum.packed)
    near_send(down_sum)
    last = [down_sum.other]
    query_sum.y_pack(*last)
    query_sum.y_send()
    query_part = contract(after(d_query_pre, *query_sum.packed), query_mat, 1, 1)
    last = [query_part]
    up_sum.far_pack(query_part)
    up_sum.far_send()
    last = up_sum.packed
    gate_sum.near_pack(*last)
    near_send(gate_sum)
    last = [gate_sum.other]
    out_sum.sum_y(*last)
    d_kv_local = after(d_kv_local, out_sum.total)
    turned = []
    for g in range(groups):
        middle = (2 * g + 1) * HD
        turned += [
            turn(d_kv_local[:, middle - HD : middle], cosine, -sine),
            d_kv_local[:, middle : middle + HD],
        ]
    d_keyvalue = jnp.concatenate(turned, axis=1).astype(bf16)

    keyvalue_sum = Reduction(attend_in, d_keyvalue)
    keyvalue_sum.core_pack()
    keyvalue_sum.core_send()
    keyvalue_part = contract(
        after(d_keyvalue, *keyvalue_sum.packed), keyvalue_mat, 1, 1
    )
    d_attend_part = query_part + keyvalue_part
    d_attend_sent = d_attend_part[half:].astype(bf16)
    got = lax.ppermute(d_attend_sent, "tensor", x_swap)
    keyvalue_sum.y_pack(d_attend_sent)
    keyvalue_sum.y_send()
    query_sum.sum_y(d_keyvalue)
    up_sum.near_pack(*keyvalue_sum.packed)
    near_send(up_sum)
    keyvalue_sum.sum_y()
    joint = jnp.concatenate([out_sum.total, query_sum.total], axis=1)
    joint = lax.psum_scatter(joint, "ctx", scatter_dimension=0, tiled=True).astype(f32)
    joint = after(joint, keyvalue_sum.total)
    out_grad, query_grad = joint[:, :query_width].T, joint[:, query_width:]
    attend_grad = keyvalue_sum.finish_ctx()

    in_factor = lax.rsqrt(jnp.mean(inputs * inputs, axis=-1, keepdims=True) + epsilon)
    pre_attend_part = jnp.sum(
        after(d_attend_part, keyvalue_sum.total) * inputs * in_factor, axis=0
    )
    gain_grads = jnp.stack([pre_attend_part, post_attend_part, pre_feed_part, post_feed_part])

    def swap_sum(values, axis, count):
        bit = 1
        while bit < count:
            pairs = [(i, i ^ bit) for i in range(count)]
            values = values + lax.ppermute(values, axis, pairs)
            bit *= 2
        return values

    gain_grads = swap_sum(gain_grads, dp_axes, dp_count)
    gain_grads = swap_sum(gain_grads, "ctx", ctx_count)
    gain_grads = swap_sum(gain_grads, "tensor", tensor_count)
    place = dp_index * ctx_count + ctx_index
    gain_grads = gain_grads.reshape(4, dp_count * ctx_count, share)
    gain_grads = lax.dynamic_slice_in_dim(gain_grads, place, 1, 1)[:, 0]

    down_grad = finish_near(down_sum.own, down_sum.got).T
    gate_grad = finish_near(gate_sum.own, gate_sum.got)
    up_grad = finish_near(up_sum.own, up_sum.got)
    key_grad = jnp.concatenate(
        [attend_grad[:, 2 * g * HD : (2 * g + 1) * HD] for g in range(groups)], axis=1
    )
    value_grad = jnp.concatenate(
        [attend_grad[:, (2 * g + 1) * HD : (2 * g + 2) * HD] for g in range(groups)], axis=1
    )

    d_attend_in = after(d_attend_part[:half], *keyvalue_sum.packed) + got.astype(f32)
    d_from_attend, _ = norm_back(own_inputs, gain_in, d_attend_in)
    input_grad = join_absolute((d_mid + d_from_attend).astype(bf16)).astype(f32)[None]

    return (
        layer_output,
        input_grad,
        gain_grads[0],
        query_grad,
        key_grad,
        value_grad,
        out_grad,
        gain_grads[1],
        gain_grads[2],
        gate_grad,
        up_grad,
        down_grad,
        gain_grads[3],
    )


def solution(mesh):
    dp_count, ctx_count, tensor_count = mesh.devices.shape
    mesh = jax.sharding.Mesh(
        mesh.devices.reshape(dp_count // cores, cores, ctx_count, tensor_count),
        ("y", "core", "ctx", "tensor"),
    )
    dp = ("y", "core")
    both = ("y", "core", "ctx")
    return jax.shard_map(
        body,
        mesh=mesh,
        in_specs=(
            P(dp, "ctx", None),
            P(dp, None),
            P(both),
            P(both, "tensor"),
            P(both, "tensor"),
            P(both, "tensor"),
            P("tensor", both),
            P(both),
            P(both),
            P(both, "tensor"),
            P(both, "tensor"),
            P("tensor", both),
            P(both),
            P(dp, "ctx", None),
        ),
        out_specs=(
            P(dp, "ctx", None),
            P(dp, "ctx", None),
            P(both),
            P(both, "tensor"),
            P(both, "tensor"),
            P(both, "tensor"),
            P("tensor", both),
            P(both),
            P(both),
            P(both, "tensor"),
            P(both, "tensor"),
            P("tensor", both),
            P(both),
        ),
        check_vma=False,
    )
```

```python
import functools

import jax
import jax.numpy as jnp
from jax import lax
from jax.experimental import pallas as pl
from jax.experimental.pallas import tpu as pltpu
from jax.sharding import PartitionSpec as P

HQ = 8
KV = 4
HD = 256
LEN = 2048

epsilon = 1e-06
cap_value = 50.0
gelu_coef = 0.7978845608028654
cores = 2
pad_lanes = 128

f32 = jnp.float32
bf16 = jnp.bfloat16


def rms_norm(values, gain):
    factor = lax.rsqrt(jnp.mean(values * values, axis=-1, keepdims=True) + epsilon)
    return values * factor * gain


def gelu_tanh(values):
    return (
        0.5 * values * (1.0 + jnp.tanh(gelu_coef * (values + 0.044715 * values * values * values)))
    )


def gated_product(gate, upward):
    return gelu_tanh(gate) * upward


def rotary_tables(positions, head_size):
    half = head_size // 2
    freqs = 10000.0 ** (-(jnp.arange(half, dtype=f32) * 2.0) / head_size)
    angle = positions.astype(f32)[:, None] * freqs[None, :]
    return (jnp.cos(angle), jnp.sin(angle))


attend_limit = 48 * 1024 * 1024


def dotted(left, right, left_dim, right_dim, precision=None):
    return lax.dot_general(
        left,
        right,
        (((left_dim,), (right_dim,)), ((), ())),
        precision=precision,
        preferred_element_type=f32,
    )


def turn(values, cosine, sine):
    half = HD // 2
    first, second = values[:, :half], values[:, half:]
    return jnp.concatenate(
        [first * cosine - second * sine, second * cosine + first * sine], axis=1
    )


def forward_kernel(chunks, pre_ref, kv_ref, cos_ref, sin_ref, qpos_ref, kpos_ref, q_ref, out_ref, low_ref, inv_ref):
    rows = pre_ref.shape[0]
    size = kv_ref.shape[0] // chunks
    q = turn(pre_ref[...], cos_ref[...], sin_ref[...]).astype(bf16)
    q_ref[...] = q
    qpos = qpos_ref[...]
    total = jnp.zeros((1, rows), f32)
    acc = jnp.zeros((HD, rows), f32)
    for c in range(chunks):
        part = pl.ds(c * size, size)
        raw = dotted(kv_ref[part, :HD], q, 1, 1)
        level = jnp.tanh(raw * (HD ** (-0.5) / cap_value))
        weight = jnp.where(qpos >= kpos_ref[part, :], jnp.exp(cap_value * level), 0.0)
        total = total + jnp.sum(weight, axis=0, keepdims=True)
        acc = acc + dotted(kv_ref[part, HD:], weight.astype(bf16), 0, 0)
    inverse = 1.0 / total
    inv_ref[0] = inverse
    out = (acc * inverse).T
    out_ref[...] = out
    low_ref[...] = out.astype(bf16)


def attend_forward(query_pre, kv_all, cosine, sine, qpos, kpos, groups, per_group, chunks):
    rows, width = query_pre.shape
    length = kv_all.shape[0]
    heads = groups * per_group
    by_head = pl.BlockSpec((rows, HD), lambda g, r: (0, g * per_group + r))
    fixed = lambda shape: pl.BlockSpec(shape, lambda g, r: (0, 0))
    return pl.pallas_call(
        functools.partial(forward_kernel, chunks),
        grid=(groups, per_group),
        in_specs=[
            by_head,
            pl.BlockSpec((length, 2 * HD), lambda g, r: (0, g)),
            fixed((rows, HD // 2)),
            fixed((rows, HD // 2)),
            fixed((1, rows)),
            fixed((length, 1)),
        ],
        out_specs=[
            by_head,
            by_head,
            by_head,
            pl.BlockSpec((1, 1, rows), lambda g, r: (g * per_group + r, 0, 0)),
        ],
        out_shape=[
            jax.ShapeDtypeStruct((rows, width), bf16),
            jax.ShapeDtypeStruct((rows, width), f32),
            jax.ShapeDtypeStruct((rows, width), bf16),
            jax.ShapeDtypeStruct((heads, 1, rows), f32),
        ],
        compiler_params=pltpu.CompilerParams(vmem_limit_bytes=attend_limit),
        cost_estimate=pl.CostEstimate(
            flops=rows * width,
            bytes_accessed=rows * width,
            transcendentals=0,
        ),
        name="attend_forward",
    )(query_pre, kv_all, cosine, sine, qpos, kpos)


def backward_kernel(per_group, q_ref, kv_ref, da_ref, out_ref, inv_ref, cos_ref, sin_ref, qpos_ref, kpos_ref, dq_ref, dkv_ref, delta_ref, sum_ref, both_ref):
    c, r = pl.program_id(1), pl.program_id(2)
    q, da = q_ref[...], da_ref[...]
    k, v = kv_ref[:, :HD], kv_ref[:, HD:]

    @pl.when(c == 0)
    def _():
        delta_ref[r] = dotted(
            jnp.ones((8, HD), f32), da.astype(f32) * out_ref[...], 1, 1, lax.Precision.HIGHEST
        )

    delta = delta_ref[r][0:1]
    level = jnp.tanh(dotted(k, q, 1, 1) * (HD ** (-0.5) / cap_value))
    seen = qpos_ref[...] >= kpos_ref[...]
    prob = jnp.where(seen, jnp.exp(cap_value * level), 0.0) * inv_ref[0]
    d_prob = dotted(v, da, 1, 1)
    d_raw = (prob * (d_prob - delta) * (1.0 - level * level)).astype(bf16)
    d_key = dotted(d_raw, q, 1, 0) * HD ** (-0.5)
    d_value = dotted(prob.astype(bf16), da, 1, 0)
    d_query = dotted(d_raw, k, 0, 0)

    @pl.when(r == 0)
    def _():
        both_ref[:, :HD] = d_key
        both_ref[:, HD:] = d_value

    @pl.when(r > 0)
    def _():
        both_ref[:, :HD] += d_key
        both_ref[:, HD:] += d_value

    @pl.when(r == per_group - 1)
    def _():
        dkv_ref[...] = both_ref[...].astype(bf16)

    @pl.when(c == 0)
    def _():
        sum_ref[r] = d_query

    @pl.when(c > 0)
    def _():
        sum_ref[r] += d_query

    for head in range(per_group):

        @pl.when((c == pl.num_programs(1) - 1) & (r == head))
        def _():
            whole = sum_ref[head] * HD ** (-0.5)
            dq_ref[:, head * HD : (head + 1) * HD] = turn(
                whole, cos_ref[...], -sin_ref[...]
            ).astype(bf16)


def attend_backward(queries, kv_all, d_attended, out, inverse, cosine, sine, qpos, kpos, groups, per_group, chunks):
    rows, width = queries.shape
    length = kv_all.shape[0]
    size = length // chunks
    heads = groups * per_group
    by_head = pl.BlockSpec((rows, HD), lambda g, c, r: (0, g * per_group + r))
    fixed = lambda shape: pl.BlockSpec(shape, lambda g, c, r: (0, 0))
    by_chunk = pl.BlockSpec((size, 2 * HD), lambda g, c, r: (c, g))
    return pl.pallas_call(
        functools.partial(backward_kernel, per_group),
        grid=(groups, chunks, per_group),
        in_specs=[
            by_head,
            by_chunk,
            by_head,
            by_head,
            pl.BlockSpec((1, 1, rows), lambda g, c, r: (g * per_group + r, 0, 0)),
            fixed((rows, HD // 2)),
            fixed((rows, HD // 2)),
            fixed((1, rows)),
            pl.BlockSpec((size, 1), lambda g, c, r: (c, 0)),
        ],
        out_specs=[
            pl.BlockSpec((rows, per_group * HD), lambda g, c, r: (0, g)),
            by_chunk,
        ],
        out_shape=[
            jax.ShapeDtypeStruct((rows, width), bf16),
            jax.ShapeDtypeStruct((length, groups * 2 * HD), bf16),
        ],
        scratch_shapes=[
            pltpu.VMEM((per_group, 8, rows), f32),
            pltpu.VMEM((per_group, rows, HD), f32),
            pltpu.VMEM((size, 2 * HD), f32),
        ],
        compiler_params=pltpu.CompilerParams(vmem_limit_bytes=attend_limit),
        cost_estimate=pl.CostEstimate(
            flops=rows * width,
            bytes_accessed=rows * width,
            transcendentals=0,
        ),
        name="attend_backward",
    )(queries, kv_all, d_attended, out, inverse, cosine, sine, qpos, kpos)


feed_limit = 56 * 1024 * 1024
feed_tile = 256


def feed_params():
    return dict(
        compiler_params=pltpu.CompilerParams(vmem_limit_bytes=feed_limit),
        cost_estimate=pl.CostEstimate(flops=1000000, bytes_accessed=1000000, transcendentals=0),
    )


def whole_block(array):
    return pl.BlockSpec(array.shape, lambda n: (0, 0))


def column_tile(array):
    return pl.BlockSpec((array.shape[0], feed_tile), lambda n: (0, n))


def row_tile(array):
    return pl.BlockSpec((feed_tile, array.shape[1]), lambda n: (n, 0))


def mix_kernel(x_ref, gate_mat_ref, up_mat_ref, gate_ref, up_ref, mixed_ref):
    x = x_ref[...]
    gate = dotted(x, gate_mat_ref[...], 1, 0)
    upward = dotted(x, up_mat_ref[...], 1, 0)
    gate_ref[...] = gate
    up_ref[...] = upward
    inner = gelu_coef * (gate + 0.044715 * gate * gate * gate)
    mixed_ref[...] = (0.5 * gate * (1.0 + jnp.tanh(inner)) * upward).astype(bf16)


def mix_forward(x, gate_mat, up_mat):
    rows, hidden = x.shape[0], gate_mat.shape[1]
    shapes = [jax.ShapeDtypeStruct((rows, hidden), kind) for kind in (f32, f32, bf16)]
    return pl.pallas_call(
        mix_kernel,
        grid=(hidden // feed_tile,),
        in_specs=[whole_block(x), column_tile(gate_mat), column_tile(up_mat)],
        out_specs=[column_tile(shape) for shape in shapes],
        out_shape=shapes,
        name="mix_forward",
        **feed_params(),
    )(x, gate_mat, up_mat)


def mix_back_kernel(d_ref, down_mat_ref, gate_ref, up_ref, d_gate_ref, d_up_ref):
    d_mixed = dotted(d_ref[...], down_mat_ref[...], 1, 0)
    gate = gate_ref[...]
    square = gate * gate
    level = jnp.tanh(gelu_coef * gate * (1.0 + 0.044715 * square))
    slope = gelu_coef * (1.0 + 3.0 * 0.044715 * square)
    curve = 0.5 * (1.0 + level)
    d_curve = curve + 0.5 * gate * (1.0 - level * level) * slope
    d_gate_ref[...] = (d_mixed * up_ref[...] * d_curve).astype(bf16)
    d_up_ref[...] = (d_mixed * (gate * curve)).astype(bf16)


def mix_backward(d_out, down_mat, gate, upward):
    shapes = [jax.ShapeDtypeStruct(gate.shape, bf16)] * 2
    return pl.pallas_call(
        mix_back_kernel,
        grid=(gate.shape[1] // feed_tile,),
        in_specs=[
            whole_block(d_out),
            column_tile(down_mat),
            column_tile(gate),
            column_tile(upward),
        ],
        out_specs=[column_tile(shape) for shape in shapes],
        out_shape=shapes,
        name="mix_backward",
        **feed_params(),
    )(d_out, down_mat, gate, upward)


def spread_kernel(count, half, *refs):
    lefts, rights, outs = refs[:count], refs[count : 2 * count], refs[2 * count :]
    total = dotted(lefts[0][...], rights[0][...], 1, 1)
    for left, right in zip(lefts[1:], rights[1:]):
        total = total + dotted(left[...], right[...], 1, 1)
    for k, out in enumerate(outs):
        out[...] = total[k * half : (k + 1) * half].astype(out.dtype)


def product_blocks(lefts, rights, half):
    rows, width = lefts[0].shape[0], rights[0].shape[0]
    shapes = [
        jax.ShapeDtypeStruct((half, width), bf16 if k else f32) for k in range(rows // half)
    ]
    return pl.pallas_call(
        functools.partial(spread_kernel, len(lefts), half),
        grid=(width // feed_tile,),
        in_specs=[whole_block(left) for left in lefts] + [row_tile(right) for right in rights],
        out_specs=[column_tile(shape) for shape in shapes],
        out_shape=shapes,
        name="product_blocks",
        **feed_params(),
    )(*lefts, *rights)


def contract(left, right, left_dim, right_dim):
    return lax.dot_general(
        left, right, (((left_dim,), (right_dim,)), ((), ())), preferred_element_type=f32
    )


def body(
    layer_input,
    block_order,
    pre_attend,
    query_weight,
    key_weight,
    value_weight,
    output_weight,
    post_attend,
    pre_feed,
    gate_weight,
    up_weight,
    down_weight,
    post_feed,
    cotangent,
):
    _, rows, width = layer_input.shape
    block_len = LEN // block_order.shape[1]
    per_group = HQ // KV
    tensor_count = lax.axis_size("tensor")
    groups = KV // tensor_count
    factor = HD ** (-0.5)
    dp_count = lax.axis_size(("y", "core"))
    ctx_count = lax.axis_size("ctx")
    tensor_index = lax.axis_index("tensor")
    ctx_index = lax.axis_index("ctx")
    dp_index = lax.axis_index(("y", "core"))
    y_count = dp_count // cores
    y_index = dp_index // cores
    core_index = dp_index % cores
    dp_axes = ("y", "core")
    share = width // (dp_count * ctx_count)
    quarter = share * ctx_count
    half = rows // tensor_count
    pair = 2
    far_count = ctx_count // pair
    far_index = ctx_index // pair
    near_index = ctx_index % pair
    x_swap = [(0, 1), (1, 0)]
    all_swaps = {}
    for bz, bx in ((0, 1), (1, 0), (1, 1)):
        all_swaps[bz, bx] = [
            (c * 2 + t, (c ^ bz) * 2 + (t ^ bx)) for c in range(ctx_count) for t in range(2)
        ]
    near_swap = [(c, c ^ 1) for c in range(ctx_count)]

    def far_shift(step):
        return [
            (c, ((c // pair + step) % far_count) * pair + c % pair) for c in range(ctx_count)
        ]

    def along(dy, dc):
        pairs = []
        for y in range(y_count):
            for core in range(cores):
                target = ((y + dy) % y_count) * cores + (core + dc) % cores
                pairs.append((y * cores + core, target))
        return pairs

    def after(value, *others):
        return lax.optimization_barrier((value, *others))[0]

    def chosen(parts, index, place):
        count = len(parts)
        result = parts[0]
        for step in range(1, count):
            result = jnp.where((index - place) % count == step, parts[step], result)
        return result

    def in_order(parts, index):
        return jnp.concatenate([chosen(parts, index, k) for k in range(len(parts))], axis=0)

    def relative(values):
        first, second = values[:half], values[half:]
        flip = tensor_index == 1
        return jnp.concatenate(
            [jnp.where(flip, second, first), jnp.where(flip, first, second)], axis=0
        )

    def join(own):
        return jnp.concatenate([own, lax.ppermute(own, "tensor", x_swap)], axis=0)

    def join_absolute(own):
        return relative(join(own))

    def join_all(own):
        parts = [own]
        for pairs in all_swaps.values():
            parts.append(lax.ppermute(own, ("ctx", "tensor"), pairs))
        return jnp.concatenate(parts, axis=0)

    def pack_all(product):
        return [product[(k + 1) * half : (k + 2) * half].astype(bf16) for k in range(3)]

    def send_all(parts):
        return [
            lax.ppermute(part, ("ctx", "tensor"), pairs)
            for part, pairs in zip(parts, all_swaps.values())
        ]

    part = half // 2

    def hop(values, bz, bx):
        return lax.ppermute(values, ("ctx", "tensor"), all_swaps[bz, bx])

    def join_by_hops(own):
        beside, below = hop(own, 0, 1), hop(own, 1, 0)
        corner = [hop(beside[:part], 1, 0), hop(below[part:], 0, 1)]
        return jnp.concatenate([own, beside, below, *corner], axis=0)

    def send_by_hops(parts):
        beside, below, corner = parts
        by_side, by_below = hop(corner[:part], 0, 1), hop(corner[part:], 1, 0)

        def joined(values, got):
            return (values.astype(f32) + got.astype(f32)).astype(bf16)

        below = jnp.concatenate([joined(below[:part], by_side), below[part:]], axis=0)
        beside = jnp.concatenate([beside[:part], joined(beside[part:], by_below)], axis=0)
        return [hop(below, 1, 0), hop(beside, 0, 1)]

    def sum_of(own, parts):
        for item in parts:
            own = own + item.astype(f32)
        return own

    all_pos = (
        block_order[0][:, None] * block_len + jnp.arange(block_len, dtype=jnp.int32)[None, :]
    ).reshape(ctx_count, tensor_count, half)
    all_pos = jnp.where(tensor_index == 1, all_pos[:, ::-1], all_pos).reshape(ctx_count, rows)
    local_pos = lax.dynamic_slice_in_dim(all_pos, ctx_index, 1, 0)[0]
    cosine, sine = rotary_tables(local_pos, HD)
    query_places = local_pos[None, :]
    key_places = all_pos.reshape(LEN, 1)

    both = ("y", "core", "ctx")
    gain_pack = jnp.stack([pre_attend, post_attend, pre_feed, post_feed], axis=1)
    gain_pack = jnp.pad(gain_pack, ((0, 0), (0, pad_lanes - 4)))
    heads_in_turn = []
    for g in range(groups):
        heads_in_turn += [
            key_weight[:, g * HD : (g + 1) * HD],
            value_weight[:, g * HD : (g + 1) * HD],
        ]
    keyvalue_pack = jnp.concatenate([*heads_in_turn, gain_pack], axis=1)
    keyvalue_all = lax.all_gather(keyvalue_pack, both, axis=0, tiled=True)
    query_pack = jnp.concatenate([query_weight, output_weight.T], axis=1)
    query_all = lax.all_gather(query_pack, both, axis=0, tiled=True)
    query_mat = query_all[:, : query_weight.shape[1]]
    out_mat = query_all[:, query_weight.shape[1] :]

    hidden = gate_weight.shape[1] // pair
    is_high = near_index == 1

    def split(weight):
        low, high = weight[:, :hidden], weight[:, hidden:]
        return jnp.where(is_high, high, low), jnp.where(is_high, low, high)

    def far_pack(mine, got):
        return jnp.concatenate(
            [jnp.where(is_high, got, mine), jnp.where(is_high, mine, got)], axis=0
        )

    def far_start(block):
        return [lax.ppermute(block, "ctx", far_shift(s)) for s in range(1, far_count)]

    gate_mine, gate_other = split(gate_weight)
    up_mine, up_other = split(up_weight)
    down_mine, down_other = split(down_weight.T)
    gate_got = lax.ppermute(gate_other, "ctx", near_swap)
    rest_got = lax.ppermute(jnp.concatenate([up_other, down_other], axis=0), "ctx", near_swap)
    gate_block = far_pack(gate_mine, gate_got)
    gate_far = far_start(gate_block)
    up_block = far_pack(up_mine, rest_got[: rest_got.shape[0] // 2])
    down_block = far_pack(down_mine, rest_got[rest_got.shape[0] // 2 :])

    query_width = query_weight.shape[1]
    keyvalue_width = 2 * key_weight.shape[1]
    keyvalue_all = after(keyvalue_all, up_block, down_block)
    keyvalue_mat = keyvalue_all[:, :keyvalue_width]
    gains = keyvalue_all[:, keyvalue_width : keyvalue_width + 8].T.astype(f32)
    gain_in, gain_out, feed_gain, feed_post = gains[0], gains[1], gains[2], gains[3]

    inputs = relative(layer_input[0].astype(f32))
    own_inputs = inputs[:half]
    cot = lax.dynamic_slice_in_dim(cotangent[0], tensor_index * half, half, 0).astype(f32)

    attend_in = rms_norm(inputs, gain_in).astype(bf16)
    keyvalue_pre = jnp.dot(attend_in, keyvalue_mat, preferred_element_type=f32)
    turned = []
    for g in range(groups):
        middle = (2 * g + 1) * HD
        turned += [
            turn(keyvalue_pre[:, middle - HD : middle], cosine, sine),
            keyvalue_pre[:, middle : middle + HD],
        ]
    kv_local = jnp.concatenate(turned, axis=1).astype(bf16)

    from_left, from_right = [kv_local], [kv_local]

    def line_step(step, left_block, right_block):
        right_pairs = [(i, i + 1) for i in range(step - 1, ctx_count - 1)]
        left_pairs = [(i, i - 1) for i in range(1, ctx_count - step + 1)]
        from_left.append(lax.ppermute(left_block, "ctx", right_pairs))
        from_right.append(lax.ppermute(right_block, "ctx", left_pairs))

    line_step(1, kv_local, kv_local)
    gate_far = [after(part, kv_local) for part in gate_far]
    gate_rows = in_order([gate_block] + gate_far, far_index)
    gate_mat = lax.all_gather(gate_rows, dp_axes, axis=0, tiled=True)
    up_far = far_start(after(up_block, gate_rows))
    for step in range(2, ctx_count):
        left_block, right_block = from_left[-1], from_right[-1]
        if step == 2:
            left_block, right_block = after(left_block, gate_rows), after(right_block, gate_rows)
        line_step(step, left_block, right_block)
    last_blocks = (from_left[-2], from_right[-2])
    query_pre = jnp.dot(
        after(attend_in, *last_blocks), query_mat, preferred_element_type=f32
    )
    kv_parts = [kv_local]
    for step in range(1, ctx_count):
        kv_parts.append(
            jnp.where(ctx_index >= step, from_left[step], from_right[ctx_count - step])
        )
    kv_all = in_order(kv_parts, ctx_index)
    up_far = [after(part, *last_blocks) for part in up_far]
    up_rows = in_order([up_block] + up_far, far_index)
    up_mat = lax.all_gather(up_rows, dp_axes, axis=0, tiled=True)
    down_far = far_start(after(down_block, up_rows))
    kv_all = after(kv_all, up_rows)
    queries, attended_wide, attended, inverse_sums = attend_forward(
        query_pre, kv_all, cosine, sine, query_places, key_places, groups, per_group, ctx_count
    )
    other = contract(attended[half:], out_mat, 1, 1).astype(bf16)
    got = lax.ppermute(other, "tensor", x_swap)
    down_far = [after(part, got) for part in down_far]
    down_rows = in_order([down_block] + down_far, far_index)
    down_mat = lax.all_gather(down_rows, dp_axes, axis=0, tiled=True)
    attend_out = contract(attended[:half], out_mat, 1, 1) + got.astype(f32)
    hidden_mid = own_inputs + rms_norm(attend_out, gain_out)
    feed_own = rms_norm(hidden_mid, feed_gain).astype(bf16)
    feed_in = join_by_hops(feed_own)
    gate, upward, mixed = mix_forward(feed_in, gate_mat, up_mat)
    feed_own, *sent = product_blocks([mixed], [down_mat], half)
    sent = send_by_hops(sent)
    feed_left = feed_in
    feed_out = sum_of(feed_own, sent)
    layer_output = join_absolute(
        (hidden_mid + rms_norm(feed_out, feed_post)).astype(bf16)
    )[None]

    class Reduction:
        def __init__(self, left, right):
            self.whole = contract(left, right, 0, 0).astype(bf16)

        def piece(self, dy, dc):
            index = ((y_index + dy) % y_count) * cores + (core_index + dc) % cores
            return lax.dynamic_slice_in_dim(self.whole, index * quarter, quarter, 0)

        def core_pack(self):
            self.packed = [self.piece(dy, 1) for dy in range(y_count)]
            return self.packed

        def core_send(self):
            self.swapped = [lax.ppermute(p, dp_axes, along(0, 1)) for p in self.packed]

        def y_pack(self, *before):
            swapped = self.swapped
            if before:
                swapped = [after(item, *before) for item in swapped]
            self.packed = [
                (self.piece(dy, 0).astype(f32) + swapped[dy].astype(f32)).astype(bf16)
                for dy in range(1, y_count)
            ]
            return self.packed

        def y_send(self):
            self.arrived = [
                lax.ppermute(p, dp_axes, along(dy + 1, 0)) for dy, p in enumerate(self.packed)
            ]

        def sum_y(self, *before):
            arrived = self.arrived
            if before:
                arrived = [after(item, *before) for item in arrived]
            total = self.piece(0, 0).astype(f32) + self.swapped[0].astype(f32)
            self.total = sum_of(total, arrived).astype(bf16)
            return self.total

        def finish_ctx(self):
            return lax.psum_scatter(
                self.total, "ctx", scatter_dimension=0, tiled=True
            ).astype(f32)

        def block_of(self, index):
            result = self.blocks[0]
            for k in range(1, far_count):
                result = jnp.where(index == k, self.blocks[k], result)
            return result

        def far_pack(self, *before):
            total = self.sum_y(*before)
            self.blocks = [
                total[k * pair * share : (k + 1) * pair * share] for k in range(far_count)
            ]
            self.packed = [
                self.block_of((far_index + step) % far_count) for step in range(1, far_count)
            ]
            return self.packed

        def far_send(self):
            self.arrived = [
                lax.ppermute(p, "ctx", far_shift(s + 1)) for s, p in enumerate(self.packed)
            ]

        def near_pack(self, *before):
            arrived = self.arrived
            if before:
                arrived = [after(item, *before) for item in arrived]
            total = sum_of(self.block_of(far_index).astype(f32), arrived)
            low, high = total[:share], total[share:]
            self.own = jnp.where(is_high, high, low)
            self.other = jnp.where(is_high, low, high).astype(bf16)
            return self.other

    CoreReduction = Reduction

    def near_send(*sums):
        sent = sums[0].other
        if len(sums) > 1:
            sent = jnp.concatenate([item.other for item in sums], axis=0)
        got = lax.ppermute(sent, "ctx", near_swap).astype(f32)
        for k, item in enumerate(sums):
            item.got = got[k * share : (k + 1) * share]

    def finish_near(own, got):
        return jnp.concatenate(
            [jnp.where(is_high, got, own), jnp.where(is_high, own, got)], axis=1
        )

    def norm_back(values, gain, incoming):
        _, back = jax.vjp(rms_norm, values, gain)
        return back(incoming)

    d_feed_out, post_feed_part = norm_back(feed_out, feed_post, cot)
    d_feed_low = join_by_hops(d_feed_out.astype(bf16))
    down_sum = Reduction(d_feed_low, mixed)
    down_sum.core_pack()
    down_sum.core_send()
    down_sum.y_pack()
    down_sum.y_send()
    d_feed_tied = after(d_feed_low, *down_sum.packed)
    d_gate, d_upward = mix_backward(d_feed_tied, down_mat, gate, upward)
    d_tied = (after(d_gate, *down_sum.packed), after(d_upward, *down_sum.packed))
    d_feed_own, *packed = product_blocks(d_tied, [gate_mat, up_mat], half)
    sent = send_all(packed)
    gate_sum = CoreReduction(after(feed_left, *packed), d_gate)
    gate_sum.core_pack()
    gate_sum.core_send()
    down_sum.far_pack(*gate_sum.packed)
    down_sum.far_send()
    up_sum = CoreReduction(after(feed_left, *down_sum.packed), d_upward)
    up_sum.core_pack()
    up_sum.core_send()
    gate_sum.y_pack(*up_sum.packed)
    gate_sum.y_send()
    own_feed = after(d_feed_own, *up_sum.packed, *gate_sum.packed)
    d_feed_in = sum_of(own_feed, sent)

    d_from_feed, pre_feed_part = norm_back(hidden_mid, feed_gain, d_feed_in)
    d_mid = cot + d_from_feed
    d_attend_out, post_attend_part = norm_back(attend_out, gain_out, d_mid)
    d_attend_own = d_attend_out.astype(bf16)
    d_attend_got = lax.ppermute(d_attend_own, "tensor", x_swap)
    up_sum.y_pack(d_attend_own)
    up_sum.y_send()
    d_attend_got = after(d_attend_got, *up_sum.packed)
    d_attend_low = jnp.concatenate([d_attend_own, d_attend_got], axis=0)
    d_attended = jnp.dot(d_attend_low, out_mat, preferred_element_type=f32).astype(bf16)
    out_sum = Reduction(after(d_attend_low, d_attended), attended)
    out_sum.core_pack()
    out_sum.core_send()
    gate_sum.far_pack(*out_sum.packed)
    gate_sum.far_send()
    d_attended = after(d_attended, *gate_sum.packed)
    d_attended = after(d_attended, *down_sum.arrived)
    d_query_pre, d_kv = attend_backward(
        queries,
        kv_all,
        d_attended,
        attended_wide,
        inverse_sums,
        cosine,
        sine,
        query_places,
        key_places,
        groups,
        per_group,
        ctx_count,
    )
    d_kv = after(d_kv, *gate_sum.arrived, *up_sum.arrived)
    d_kv_local = lax.psum_scatter(d_kv, "ctx", scatter_dimension=0, tiled=True).astype(f32)
    out_sum.y_pack(d_kv)
    out_sum.y_send()
    query_sum = Reduction(after(attend_in, *out_sum.packed), d_query_pre)
    query_sum.core_pack()
    query_sum.core_send()
    last = query_sum.packed
    down_sum.near_pack(*query_sum.packed)
    near_send(down_sum)
    last = [down_sum.other]
    up_sum.far_pack(*last)
    up_sum.far_send()
    query_sum.y_pack(*up_sum.packed)
    query_sum.y_send()
    query_part = contract(after(d_query_pre, *query_sum.packed), query_mat, 1, 1)
    last = [query_part]
    gate_sum.near_pack(*last)
    near_send(gate_sum)
    last = [gate_sum.other]
    out_sum.sum_y(*last)
    d_kv_local = after(d_kv_local, out_sum.total)
    turned = []
    for g in range(groups):
        middle = (2 * g + 1) * HD
        turned += [
            turn(d_kv_local[:, middle - HD : middle], cosine, -sine),
            d_kv_local[:, middle : middle + HD],
        ]
    d_keyvalue = jnp.concatenate(turned, axis=1).astype(bf16)

    keyvalue_sum = Reduction(attend_in, d_keyvalue)
    keyvalue_sum.core_pack()
    keyvalue_sum.core_send()
    keyvalue_part = contract(
        after(d_keyvalue, *keyvalue_sum.packed), keyvalue_mat, 1, 1
    )
    d_attend_part = query_part + keyvalue_part
    d_attend_sent = d_attend_part[half:].astype(bf16)
    got = lax.ppermute(d_attend_sent, "tensor", x_swap)
    keyvalue_sum.y_pack(d_attend_sent)
    keyvalue_sum.y_send()
    query_sum.sum_y(d_keyvalue)
    up_sum.near_pack(*keyvalue_sum.packed)
    near_send(up_sum)
    keyvalue_sum.sum_y()
    joint = jnp.concatenate([out_sum.total, query_sum.total], axis=1)
    joint = lax.psum_scatter(joint, "ctx", scatter_dimension=0, tiled=True).astype(f32)
    joint = after(joint, keyvalue_sum.total)
    out_grad, query_grad = joint[:, :query_width].T, joint[:, query_width:]
    attend_grad = keyvalue_sum.finish_ctx()

    in_factor = lax.rsqrt(jnp.mean(inputs * inputs, axis=-1, keepdims=True) + epsilon)
    pre_attend_part = jnp.sum(
        after(d_attend_part, keyvalue_sum.total) * inputs * in_factor, axis=0
    )
    gain_grads = jnp.stack([pre_attend_part, post_attend_part, pre_feed_part, post_feed_part])

    def swap_sum(values, axis, count):
        bit = 1
        while bit < count:
            pairs = [(i, i ^ bit) for i in range(count)]
            values = values + lax.ppermute(values, axis, pairs)
            bit *= 2
        return values

    gain_grads = swap_sum(gain_grads, dp_axes, dp_count)
    gain_grads = swap_sum(gain_grads, "ctx", ctx_count)
    gain_grads = swap_sum(gain_grads, "tensor", tensor_count)
    place = dp_index * ctx_count + ctx_index
    gain_grads = gain_grads.reshape(4, dp_count * ctx_count, share)
    gain_grads = lax.dynamic_slice_in_dim(gain_grads, place, 1, 1)[:, 0]

    down_grad = finish_near(down_sum.own, down_sum.got).T
    gate_grad = finish_near(gate_sum.own, gate_sum.got)
    up_grad = finish_near(up_sum.own, up_sum.got)
    key_grad = jnp.concatenate(
        [attend_grad[:, 2 * g * HD : (2 * g + 1) * HD] for g in range(groups)], axis=1
    )
    value_grad = jnp.concatenate(
        [attend_grad[:, (2 * g + 1) * HD : (2 * g + 2) * HD] for g in range(groups)], axis=1
    )

    d_attend_in = after(d_attend_part[:half], *keyvalue_sum.packed) + got.astype(f32)
    d_from_attend, _ = norm_back(own_inputs, gain_in, d_attend_in)
    input_grad = join_absolute((d_mid + d_from_attend).astype(bf16)).astype(f32)[None]

    return (
        layer_output,
        input_grad,
        gain_grads[0],
        query_grad,
        key_grad,
        value_grad,
        out_grad,
        gain_grads[1],
        gain_grads[2],
        gate_grad,
        up_grad,
        down_grad,
        gain_grads[3],
    )


def solution(mesh):
    dp_count, ctx_count, tensor_count = mesh.devices.shape
    mesh = jax.sharding.Mesh(
        mesh.devices.reshape(dp_count // cores, cores, ctx_count, tensor_count),
        ("y", "core", "ctx", "tensor"),
    )
    dp = ("y", "core")
    both = ("y", "core", "ctx")
    return jax.shard_map(
        body,
        mesh=mesh,
        in_specs=(
            P(dp, "ctx", None),
            P(dp, None),
            P(both),
            P(both, "tensor"),
            P(both, "tensor"),
            P(both, "tensor"),
            P("tensor", both),
            P(both),
            P(both),
            P(both, "tensor"),
            P(both, "tensor"),
            P("tensor", both),
            P(both),
            P(dp, "ctx", None),
        ),
        out_specs=(
            P(dp, "ctx", None),
            P(dp, "ctx", None),
            P(both),
            P(both, "tensor"),
            P(both, "tensor"),
            P(both, "tensor"),
            P("tensor", both),
            P(both),
            P(both),
            P(both, "tensor"),
            P(both, "tensor"),
            P("tensor", both),
            P(both),
        ),
        check_vma=False,
    )
```
